128 devices in a mesh: smp: 8 (over x_lo, z), bld: 16 (over y, x_hi, core).
Axes of the slice: x: 4 (x_hi: 2, x_lo: 2; x = x_hi * 2 + x_lo), y: 4, z: 4, core: 2. Of those that a mesh axis runs over, the one named last changes fastest.
Arguments:
- tensor: bfloat16 [4, 8192, 16384], P(None, 'smp', 'bld'), may hold values from -576 to 576
- building_factor: float32 [64, 16384], P(None, 'bld'), may hold values from -144 to 144
- hour_weights: float32 [4, 64], replicated, may hold values from -5 to 5
Outputs:
- sample_factor: float32 [64, 8192], P(None, ('smp', 'bld'))
- building_out: float32 [64, 16384], P(None, ('bld', 'smp'))
- hour_out: float32 [4, 64], replicated
The draws below stay inside these ranges and needn't reach their ends.
All inputs are finite; a program needn't handle non-finite values.
Results may differ from the reference program's by a relative error of at most 0.008.
Values may be sent and summed in bfloat16 or wider, within the bound.
A program may use at most 64 MiB of HBM per device.

```python
import math
import jax
import jax.numpy as jnp
from jax import lax

R = 64
HOURS = 4
SWEEPS = 5
SAMPLES = 8192
BUILDINGS = 16384


def rising_scale(count, key):
    position = jnp.arange(count, dtype=jnp.float32) / max(count - 1, 1)
    return (1.0 + 2.0 * position) * jnp.exp(jax.random.uniform(key, (count,), jnp.float32) * math.log(4.0))


def draw_tensor(key, part):
    key_noise = jax.random.fold_in(key, 11)
    key_rows = jax.random.fold_in(key, 12)
    key_cols = jax.random.fold_in(key, 13)
    noise_part = jnp.clip(jax.random.normal(key_noise, (HOURS, SAMPLES, BUILDINGS), jnp.float32), -4.0, 4.0)
    values = noise_part * rising_scale(SAMPLES, key_rows)[None, :, None] * rising_scale(BUILDINGS, key_cols)[None, None, :]
    return values.astype(jnp.bfloat16)


def draw_building_factor(key, part):
    key_noise = jax.random.fold_in(key, 21)
    key_cols = jax.random.fold_in(key, 22)
    key_rank = jax.random.fold_in(key, 23)
    noise_part = jnp.clip(jax.random.normal(key_noise, (R, BUILDINGS), jnp.float32), -4.0, 4.0)
    rank_scale = jnp.exp(jax.random.uniform(key_rank, (R,), jnp.float32) * math.log(3.0))
    values = noise_part * rising_scale(BUILDINGS, key_cols)[None, :] * rank_scale[:, None]
    return values.astype(jnp.float32)


def noise(stream_key, dims, deviation, bound, kind=jnp.bfloat16):
    entries = jax.random.normal(stream_key, dims, jnp.float32) * deviation
    return jnp.minimum(jnp.maximum(entries, -bound), bound).astype(kind)


def setup_inputs(seed: int = 0) -> dict:
    seeds = jax.random.split(jax.random.key(seed), 4)
    return {
        "tensor": draw_tensor(jax.random.fold_in(seeds[3], 71), 0),
        "building_factor": draw_building_factor(jax.random.fold_in(seeds[3], 71), 0),
        "hour_weights": noise(seeds[2], (HOURS, R), 1.0, 5.0, jnp.float32),
    }


EPSILON = 1e-06
RIDGE_SHARE = 0.05

def regularized(gram):
    order_size = gram.shape[0]
    return gram + RIDGE_SHARE * jnp.mean(jnp.diagonal(gram)) * jnp.eye(order_size, dtype=gram.dtype)

def solve_rows(gram, right_side):
    lower_factor = jnp.linalg.cholesky(regularized(gram))
    middle = lax.linalg.triangular_solve(lower_factor, right_side, left_side=True, lower=True)
    return lax.linalg.triangular_solve(lower_factor, middle, left_side=True, lower=True, transpose_a=True)

def finish(unscaled, gram_raw, row_count):
    column_norm = jnp.sqrt(jnp.diagonal(gram_raw) / row_count + EPSILON)
    return (unscaled / column_norm[:, None], gram_raw / (column_norm[:, None] * column_norm[None, :]))

def hour_gram(hourly):
    return jnp.dot(hourly.T, hourly, precision=lax.Precision.HIGHEST)

def reference(tensor, building_factor, hour_weights):
    scale_up = math.sqrt(SAMPLES * BUILDINGS)
    hourly = hour_weights / scale_up
    gram_build = jnp.dot(building_factor, building_factor.T, precision=lax.Precision.HIGHEST)
    build_low = building_factor.astype(jnp.bfloat16)

    def project(build_now):

        def one_hour(hour_slab):
            return lax.dot_general(build_now.astype(jnp.float32), hour_slab.astype(jnp.float32), (((1,), (1,)), ((), ())), preferred_element_type=jnp.float32)
        return lax.map(one_hour, tensor)
    partial_value = project(build_low)
    samples_now = None
    building_now = building_factor
    for sweep_index in range(SWEEPS):
        sample_rhs = lax.optimization_barrier(jnp.sum(hourly[:, :, None] * partial_value, axis=0))
        unscaled = solve_rows(gram_build * hour_gram(hourly), sample_rhs)
        gram_raw = jnp.dot(unscaled, unscaled.T, precision=lax.Precision.HIGHEST)
        samples_now, gram_sample = finish(unscaled, gram_raw, SAMPLES)
        sample_low = samples_now.astype(jnp.bfloat16)

        def one_mixed(hour_slab):
            return lax.dot_general(sample_low.astype(jnp.float32), hour_slab.astype(jnp.float32), (((1,), (0,)), ((), ())), preferred_element_type=jnp.float32)
        mixed = lax.map(one_mixed, tensor)
        build_rhs = lax.optimization_barrier(jnp.sum(hourly[:, :, None] * mixed, axis=0))
        unscaled = solve_rows(gram_sample * hour_gram(hourly), build_rhs)
        gram_raw = jnp.dot(unscaled, unscaled.T, precision=lax.Precision.HIGHEST)
        building_now, gram_build = finish(unscaled, gram_raw, BUILDINGS)
        build_low = building_now.astype(jnp.bfloat16)
        partial_value = project(build_low)
        hour_rhs = lax.optimization_barrier(jnp.sum(sample_low.astype(jnp.float32)[None, :, :] * partial_value, axis=2))
        hourly = solve_rows(gram_sample * gram_build, hour_rhs.T).T
    return (samples_now, building_now, hourly * scale_up)
```

```python
import functools
import math

import jax
import jax.numpy as jnp
from jax import lax
from jax.experimental import pallas as pl
from jax.experimental.pallas import tpu as pltpu
from jax.sharding import PartitionSpec as P

SWEEPS = 5
EPSILON = 1e-06
RIDGE_SHARE = 0.05
HIGHEST = lax.Precision.HIGHEST
MESH = pl.DeviceIdType.MESH
NT = (((1,), (1,)), ((), ()))
NN = (((1,), (0,)), ((), ()))

BLD_STEPS = [
    (dy, dx, dc) for dy in (2, 1, 3, 0) for dx in (1, 0) for dc in (1, 0) if (dy, dx, dc) != (0, 0, 0)
]
SMP_STEPS = [(dx, dz) for dz in (2, 1, 3, 0) for dx in (1, 0) if (dx, dz) != (0, 0)]


def dot32(a, b, dims=NN):
    return lax.dot_general(a, b, dims, precision=HIGHEST, preferred_element_type=jnp.float32)


def dot16(a, b, dims=NN):
    return lax.dot_general(a, b, dims, preferred_element_type=jnp.float32)


def identity(n):
    rows = lax.broadcasted_iota(jnp.int32, (n, n), 0)
    cols = lax.broadcasted_iota(jnp.int32, (n, n), 1)
    return (rows == cols).astype(jnp.float32)


def pack(square):
    half = square.shape[0] // 2
    return jnp.concatenate([square[:half], square[half:]], axis=1)


def unpack(packed):
    half = packed.shape[1] // 2
    return jnp.concatenate([packed[:, :half], packed[:, half:]], axis=0)


def regularized_inverse(gram):
    n = gram.shape[0]
    eye = identity(n)
    mean = jnp.sum(jnp.sum(gram * eye, axis=0, keepdims=True), axis=1, keepdims=True) / n
    scale = 2.0 / ((n + 2 * RIDGE_SHARE) * mean)
    first = scale * (gram + RIDGE_SHARE * mean * eye)
    spread = n / (n + 2 * RIDGE_SHARE)
    t = first
    y = None
    steps = 7
    for step in range(steps):
        spread = spread * spread / (2.0 - spread * spread)
        gain = 1.0 + spread
        factor = gain * (2.0 * eye - t)
        if step == 0:
            y = factor
            t = dot32(t, factor)
        elif step < steps - 1:
            both = dot32(jnp.concatenate([y, t], axis=0), factor)
            y, t = both[:n], both[n:]
        else:
            y = dot32(y, factor)
    residual = eye - dot32(first, y)
    y = y + dot32(y, residual)
    return scale * y


def scales_of(gram_raw, count):
    eye = identity(gram_raw.shape[0])
    diag_row = jnp.sum(gram_raw * eye, axis=0, keepdims=True)
    diag_col = jnp.sum(gram_raw * eye, axis=1, keepdims=True)
    inv_row = 1.0 / jnp.sqrt(diag_row / count + EPSILON)
    inv_col = 1.0 / jnp.sqrt(diag_col / count + EPSILON)
    return inv_row, inv_col


def kernel(
    n_smp, n_bld, samples_total, buildings_total,
    tensor_ref, build_ref, hour_ref,
    sample_out, build_out, hour_out,
    slab, partial, mixed, factor, us_slice, ub_slice,
    gram_build, gram_sample, hour_rows, hour_cols, inv_b_col, inv_s_row, inv_s_col, gram_tmp,
    rs1_send, rs1_recv, ag1_send, ag1_recv, gs_send, gs_recv,
    rs2_send, rs2_recv, ag2_send, ag2_recv, p1_send, p1_recv, p2_send, p2_recv,
    load_sem, send_sems, recv_sems,
):
    hours, n_i, n_j = slab.shape
    rank = build_ref.shape[0]
    scale_up = math.sqrt(samples_total * buildings_total)
    smp = lax.axis_index("smp")
    bld = lax.axis_index("bld")
    core = bld % 2
    x_hi = (bld // 2) % 2
    y = bld // 4
    z = smp % 4
    x_lo = smp // 4

    def bld_peer(step):
        dy, dx, dc = step
        return ((y + dy) % 4) * 4 + ((x_hi + dx) % 2) * 2 + (core + dc) % 2

    def smp_peer(step):
        dx, dz = step
        return ((x_lo + dx) % 2) * 4 + (z + dz) % 4

    bld_peers = [bld_peer(step) for step in BLD_STEPS]
    smp_peers = [smp_peer(step) for step in SMP_STEPS]

    def start_exchange(axis, sem, piece_of, recv):
        peers, me = (bld_peers, bld) if axis == "bld" else (smp_peers, smp)
        for peer in peers:
            pltpu.make_async_remote_copy(
                src_ref=piece_of(peer),
                dst_ref=recv.at[me],
                send_sem=send_sems.at[sem],
                recv_sem=recv_sems.at[sem],
                device_id={axis: peer},
                device_id_type=MESH,
            ).start()

    def finish_exchange(sem, recv):
        others = recv.at[pl.ds(0, recv.shape[0] - 1)]
        done = pltpu.make_async_remote_copy(
            src_ref=others,
            dst_ref=others,
            send_sem=send_sems.at[sem],
            recv_sem=recv_sems.at[sem],
            device_id={"bld": bld_peers[0]},
            device_id_type=MESH,
        )
        done.wait_recv()
        done.wait_send()

    barrier = pltpu.get_barrier_semaphore()
    for peer in bld_peers:
        pl.semaphore_signal(barrier, inc=1, device_id={"bld": peer}, device_id_type=MESH)
    for peer in smp_peers:
        pl.semaphore_signal(barrier, inc=1, device_id={"smp": peer}, device_id_type=MESH)

    def load(k):
        return pltpu.make_async_copy(tensor_ref.at[k], slab.at[k], load_sem.at[k])

    for k in range(hours):
        load(k).start()

    tile = 512

    def project(k):
        for i in range(0, n_i, tile):
            partial[k, :, i : i + tile] = dot16(factor[...], slab[k, i : i + tile, :], NT)

    def mix(k):
        for j in range(0, n_j, tile):
            mixed[k, :, j : j + tile] = dot16(factor[...], slab[k, :, j : j + tile], NN)

    def share_start(gram, hour_terms):
        gram_tmp[...] = gram
        rows = rank // n_smp
        mine = gram_tmp[pl.ds(pl.multiple_of(smp * rows, rows), rows), :]
        message = jnp.concatenate([mine, hour_terms], axis=1)
        p1_send[...] = message
        p1_recv[bld] = message
        start_exchange("bld", 5, lambda peer: p1_send, p1_recv)

    def share_finish():
        finish_exchange(5, p1_recv)
        total = p1_recv[0]
        for b in range(1, n_bld):
            total = total + p1_recv[b]
        p2_send[...] = total
        p2_recv[smp] = total
        start_exchange("smp", 6, lambda peer: p2_send, p2_recv)
        finish_exchange(6, p2_recv)
        gram = p2_recv[...].reshape(rank, 2 * rank)[:, :rank]
        hour_sum = p2_recv[0][:, rank:]
        for s in range(1, n_smp):
            hour_sum = hour_sum + p2_recv[s][:, rank:]
        return gram, hour_sum

    pad = hour_rows.shape[0]
    rows_k = lax.broadcasted_iota(jnp.int32, (pad, hours * 128), 0)
    lanes_k = lax.broadcasted_iota(jnp.int32, (pad, hours * 128), 1)
    pick = (rows_k == lanes_k // 128).astype(jnp.float32)

    hour_rows[...] = jnp.zeros_like(hour_rows)
    hour_rows[0:hours, :] = hour_ref[...] / scale_up
    hour_cols[...] = dot32(identity(rank), hour_rows[...], NT)
    inv_b_col[...] = jnp.ones_like(inv_b_col)
    start_factor = build_ref[...]
    factor[...] = start_factor.astype(jnp.bfloat16)
    gram0 = dot32(start_factor, start_factor, NT)

    pl.semaphore_wait(barrier, n_bld + n_smp - 2)
    share_start(gram0, jnp.zeros((rank // n_smp, rank), jnp.float32))
    for k in range(hours):
        load(k).wait()
        project(k)
    gram, _ = share_finish()
    gram_build[...] = gram

    @pl.loop(0, SWEEPS)
    def _(sweep):
        gram_hour = dot32(hour_cols[...], hour_rows[...])

        half = rank // 2
        lane = lax.broadcasted_iota(jnp.int32, (half, 128), 1)
        low_lane = lane < 64
        cols = [
            jnp.broadcast_to(hour_cols[:, k : k + 1] * inv_b_col[:, 0:1], (rank, 128))
            for k in range(hours)
        ]
        for m in range(n_bld // 2):
            block = cols[0] * partial[0, :, m * 128 : (m + 1) * 128]
            for k in range(1, hours):
                block = block + cols[k] * partial[k, :, m * 128 : (m + 1) * 128]
            top, low = block[:half], block[half:]
            rs1_send[2 * m] = jnp.where(low_lane, top, pltpu.roll(low, 64, 1)).astype(rs1_send.dtype)
            rs1_send[2 * m + 1] = jnp.where(low_lane, pltpu.roll(top, 64, 1), low).astype(rs1_send.dtype)
        rs1_recv[bld] = rs1_send[bld]
        start_exchange("bld", 0, lambda peer: rs1_send.at[peer], rs1_recv)
        inverse = regularized_inverse(gram_build[...] * gram_hour)
        finish_exchange(0, rs1_recv)
        total = rs1_recv[0].astype(jnp.float32)
        for b in range(1, n_bld):
            total = total + rs1_recv[b].astype(jnp.float32)
        unscaled = dot32(inverse, unpack(total))
        us_slice[...] = unscaled
        message = pack(unscaled).astype(jnp.bfloat16)
        ag1_send[...] = message
        ag1_recv[bld] = message
        start_exchange("bld", 1, lambda peer: ag1_send, ag1_recv)
        finish_exchange(1, ag1_recv)
        for m in range(n_bld // 2):
            even = ag1_recv[2 * m].astype(jnp.float32)
            odd = ag1_recv[2 * m + 1].astype(jnp.float32)
            top = jnp.where(low_lane, even, pltpu.roll(odd, 64, 1))
            low = jnp.where(low_lane, pltpu.roll(even, 64, 1), odd)
            factor[0:half, m * 128 : (m + 1) * 128] = top.astype(jnp.bfloat16)
            factor[half:rank, m * 128 : (m + 1) * 128] = low.astype(jnp.bfloat16)

        gram_part = pack(dot16(factor[...], factor[...], NT))
        gs_send[...] = gram_part
        gs_recv[smp] = gram_part
        start_exchange("smp", 2, lambda peer: gs_send, gs_recv)

        @pl.loop(0, hours)
        def _(k):
            mix(k)

        cols = [jnp.broadcast_to(hour_cols[:, k : k + 1], (rank, 128)) for k in range(hours)]
        for s in range(n_smp):
            block = cols[0] * mixed[0, :, s * 128 : (s + 1) * 128]
            for k in range(1, hours):
                block = block + cols[k] * mixed[k, :, s * 128 : (s + 1) * 128]
            rs2_send[s] = block.astype(rs2_send.dtype)
        rs2_recv[smp] = rs2_send[smp]
        start_exchange("smp", 3, lambda peer: rs2_send.at[peer], rs2_recv)

        finish_exchange(2, gs_recv)
        gram_raw = gs_recv[0]
        for s in range(1, n_smp):
            gram_raw = gram_raw + gs_recv[s]
        gram_raw = unpack(gram_raw)
        inv_row, inv_col = scales_of(gram_raw, samples_total)
        inv_s_row[...] = jnp.broadcast_to(inv_row, inv_s_row.shape)
        inv_s_col[...] = jnp.broadcast_to(inv_col, inv_s_col.shape)
        gram_sample[...] = gram_raw * (inv_col * inv_row)
        inverse = regularized_inverse(gram_sample[...] * gram_hour) * inv_row

        finish_exchange(3, rs2_recv)
        total = rs2_recv[0].astype(jnp.float32)
        for s in range(1, n_smp):
            total = total + rs2_recv[s].astype(jnp.float32)
        unscaled = dot32(inverse, total)
        ub_slice[...] = unscaled
        message = unscaled.astype(jnp.bfloat16)
        ag2_send[...] = message
        ag2_recv[smp] = message
        start_exchange("smp", 4, lambda peer: ag2_send, ag2_recv)
        finish_exchange(4, ag2_recv)
        for s in range(n_smp):
            factor[:, s * 128 : (s + 1) * 128] = ag2_recv[s]

        sums = []
        for k in range(hours):
            acc = jnp.zeros((rank, 128), jnp.float32)
            for s in range(n_smp):
                acc = acc + mixed[k, :, s * 128 : (s + 1) * 128] * ag2_recv[s].astype(jnp.float32)
            sums.append(acc)
        hour_terms = dot32(pick, jnp.concatenate(sums, axis=1), NT)
        share_start(dot16(factor[...], factor[...], NT), hour_terms)

        @pl.loop(0, hours)
        def _(k):
            project(k)

        gram_raw, hour_sum = share_finish()
        inv_row, inv_col = scales_of(gram_raw, buildings_total)
        inv_b_col[...] = jnp.broadcast_to(inv_col, inv_b_col.shape)
        gram_build[...] = gram_raw * (inv_col * inv_row)
        hour_rhs = hour_sum * (inv_row * inv_s_row[0:1, :])
        inverse = regularized_inverse(gram_sample[...] * gram_build[...])
        hour_rows[...] = dot32(hour_rhs, inverse)
        hour_cols[...] = dot32(inverse, hour_rhs, NT)

    sample_out[...] = us_slice[...] * inv_s_col[:, 0:1]
    build_out[...] = ub_slice[...] * inv_b_col[:, 0:1]
    hour_out[...] = hour_rows[0:hours, :] * scale_up


def local(tensor, building_factor, hour_weights):
    n_smp = lax.axis_size("smp")
    n_bld = lax.axis_size("bld")
    hours, n_i, n_j = tensor.shape
    rank = building_factor.shape[0]
    assert (n_smp, n_bld, rank, hours) == (8, 16, 64, 4)
    i_share, j_share = n_i // n_bld, n_j // n_smp
    assert (i_share, j_share) == (64, 128)
    f32, bf16 = jnp.float32, jnp.bfloat16
    body = functools.partial(kernel, n_smp, n_bld, n_i * n_smp, n_j * n_bld)
    vmem = pl.BlockSpec(memory_space=pltpu.VMEM)
    pad = 8
    return pl.pallas_call(
        body,
        out_shape=(
            jax.ShapeDtypeStruct((rank, i_share), f32),
            jax.ShapeDtypeStruct((rank, j_share), f32),
            jax.ShapeDtypeStruct((hours, rank), f32),
        ),
        in_specs=[pl.BlockSpec(memory_space=pl.ANY), vmem, vmem],
        out_specs=(vmem, vmem, vmem),
        scratch_shapes=[
            pltpu.VMEM((hours, n_i, n_j), bf16),
            pltpu.VMEM((hours, rank, n_i), f32),
            pltpu.VMEM((hours, rank, n_j), f32),
            pltpu.VMEM((rank, n_j), bf16),
            pltpu.VMEM((rank, i_share), f32),
            pltpu.VMEM((rank, j_share), f32),
            pltpu.VMEM((rank, rank), f32),
            pltpu.VMEM((rank, rank), f32),
            pltpu.VMEM((pad, rank), f32),
            pltpu.VMEM((rank, pad), f32),
            pltpu.VMEM((rank, pad), f32),
            pltpu.VMEM((pad, rank), f32),
            pltpu.VMEM((rank, pad), f32),
            pltpu.VMEM((rank, rank), f32),
            pltpu.VMEM((n_bld, rank // 2, 2 * i_share), bf16),
            pltpu.VMEM((n_bld, rank // 2, 2 * i_share), bf16),
            pltpu.VMEM((rank // 2, 2 * i_share), bf16),
            pltpu.VMEM((n_bld, rank // 2, 2 * i_share), bf16),
            pltpu.VMEM((rank // 2, 2 * rank), f32),
            pltpu.VMEM((n_smp, rank // 2, 2 * rank), f32),
            pltpu.VMEM((n_smp, rank, j_share), bf16),
            pltpu.VMEM((n_smp, rank, j_share), bf16),
            pltpu.VMEM((rank, j_share), bf16),
            pltpu.VMEM((n_smp, rank, j_share), bf16),
            pltpu.VMEM((rank // n_smp, 2 * rank), f32),
            pltpu.VMEM((n_bld, rank // n_smp, 2 * rank), f32),
            pltpu.VMEM((rank // n_smp, 2 * rank), f32),
            pltpu.VMEM((n_smp, rank // n_smp, 2 * rank), f32),
            pltpu.SemaphoreType.DMA((hours,)),
            pltpu.SemaphoreType.DMA((7,)),
            pltpu.SemaphoreType.DMA((7,)),
        ],
        compiler_params=pltpu.CompilerParams(
            collective_id=0, has_side_effects=True, vmem_limit_bytes=40 * 1024 * 1024
        ),
        name="als_sweeps",
    )(tensor, building_factor, hour_weights)


def solution(mesh):
    in_specs = (P(None, "smp", "bld"), P(None, "bld"), P())
    out_specs = (P(None, ("smp", "bld")), P(None, ("bld", "smp")), P())
    return jax.shard_map(local, mesh=mesh, in_specs=in_specs, out_specs=out_specs, check_vma=False)
```

```python
import functools
import math

import jax
import jax.numpy as jnp
from jax import lax
from jax.experimental import pallas as pl
from jax.experimental.pallas import tpu as pltpu
from jax.sharding import PartitionSpec as P

SWEEPS = 5
EPSILON = 1e-06
RIDGE_SHARE = 0.05
HIGHEST = lax.Precision.HIGHEST
MESH = pl.DeviceIdType.MESH
NT = (((1,), (1,)), ((), ()))
NN = (((1,), (0,)), ((), ()))

BLD_STEPS = [
    (dy, dx, dc) for dy in (2, 1, 3, 0) for dx in (1, 0) for dc in (1, 0) if (dy, dx, dc) != (0, 0, 0)
]
SMP_STEPS = [(dx, dz) for dz in (2, 1, 3, 0) for dx in (1, 0) if (dx, dz) != (0, 0)]


def dot32(a, b, dims=NN):
    return lax.dot_general(a, b, dims, precision=HIGHEST, preferred_element_type=jnp.float32)


def dot16(a, b, dims=NN):
    return lax.dot_general(a, b, dims, preferred_element_type=jnp.float32)


def identity(n):
    rows = lax.broadcasted_iota(jnp.int32, (n, n), 0)
    cols = lax.broadcasted_iota(jnp.int32, (n, n), 1)
    return (rows == cols).astype(jnp.float32)


def pack(square):
    half = square.shape[0] // 2
    return jnp.concatenate([square[:half], square[half:]], axis=1)


def unpack(packed):
    half = packed.shape[1] // 2
    return jnp.concatenate([packed[:, :half], packed[:, half:]], axis=0)


def regularized_inverse(gram):
    n = gram.shape[0]
    eye = identity(n)
    mean = jnp.sum(jnp.sum(gram * eye, axis=0, keepdims=True), axis=1, keepdims=True) / n
    scale = 2.0 / ((n + 2 * RIDGE_SHARE) * mean)
    t = scale * (gram + RIDGE_SHARE * mean * eye)
    y = None
    spread = n / (n + 2 * RIDGE_SHARE)
    steps = 8
    for step in range(steps):
        spread = spread * spread / (2.0 - spread * spread)
        gain = 1.0 + spread
        factor = gain * (2.0 * eye - t)
        if step == 0:
            y = factor
            t = dot32(t, factor)
        elif step < steps - 1:
            both = dot32(jnp.concatenate([y, t], axis=0), factor)
            y, t = both[:n], both[n:]
        else:
            y = dot32(y, factor)
    return scale * y


def three_parts(x):
    high = x.astype(jnp.bfloat16)
    rest = x - high.astype(jnp.float32)
    middle = rest.astype(jnp.bfloat16)
    low = (rest - middle.astype(jnp.float32)).astype(jnp.bfloat16)
    return jnp.concatenate([high, middle, low], axis=0)


def scales_of(gram_raw, count):
    eye = identity(gram_raw.shape[0])
    diag_row = jnp.sum(gram_raw * eye, axis=0, keepdims=True)
    diag_col = jnp.sum(gram_raw * eye, axis=1, keepdims=True)
    inv_row = 1.0 / jnp.sqrt(diag_row / count + EPSILON)
    inv_col = 1.0 / jnp.sqrt(diag_col / count + EPSILON)
    return inv_row, inv_col


RS1, AG1, GS, RS2, AG2, GB, P1, P2, COUNT = 0, 4, 8, 9, 10, 11, 12, 13, 14


def kernel(
    n_smp, n_bld, samples_total, buildings_total,
    tensor_ref, build_ref, hour_ref,
    sample_out, build_out, hour_out,
    slab, mixed, factor, s_slice, ub_slice,
    gram_build, gram_sample, inv_sample, hour_rows, hour_cols, inv_b_col, inv_s_row, inv_s_col,
    rs1_send, rs1_recv, ag1_send, ag1_recv, gs_send, gs_recv,
    rs2_send, rs2_recv, ag2_send, ag2_recv, gb_send, gb_recv, p1_send, p1_recv, p2_send, p2_recv,
    load_sem, send_sems, recv_sems,
):
    hours, n_i, n_j = slab.shape
    rank = build_ref.shape[0]
    half = rank // 2
    scale_up = math.sqrt(samples_total * buildings_total)
    smp = lax.axis_index("smp")
    bld = lax.axis_index("bld")
    core = bld % 2
    x_hi = (bld // 2) % 2
    y = bld // 4
    z = smp % 4
    x_lo = smp // 4

    def bld_peer(step):
        dy, dx, dc = step
        return ((y + dy) % 4) * 4 + ((x_hi + dx) % 2) * 2 + (core + dc) % 2

    def smp_peer(step):
        dx, dz = step
        return ((x_lo + dx) % 2) * 4 + (z + dz) % 4

    bld_peers = [bld_peer(step) for step in BLD_STEPS]
    smp_peers = [smp_peer(step) for step in SMP_STEPS]

    def start_exchange(axis, piece_of, place, sem_of):
        peers, steps = (bld_peers, BLD_STEPS) if axis == "bld" else (smp_peers, SMP_STEPS)
        for peer, step in zip(peers, steps):
            pltpu.make_async_remote_copy(
                src_ref=piece_of(peer),
                dst_ref=place,
                send_sem=send_sems.at[sem_of(step)],
                recv_sem=recv_sems.at[sem_of(step)],
                device_id={axis: peer},
                device_id_type=MESH,
            ).start()

    def finish_exchange(sem, pieces):
        done = pltpu.make_async_remote_copy(
            src_ref=pieces,
            dst_ref=pieces,
            send_sem=send_sems.at[sem],
            recv_sem=recv_sems.at[sem],
            device_id={"bld": bld_peers[0]},
            device_id_type=MESH,
        )
        done.wait_recv()
        done.wait_send()

    barrier = pltpu.get_barrier_semaphore()
    for peer in bld_peers:
        pl.semaphore_signal(barrier, inc=1, device_id={"bld": peer}, device_id_type=MESH)
    for peer in smp_peers:
        pl.semaphore_signal(barrier, inc=1, device_id={"smp": peer}, device_id_type=MESH)

    def load(k):
        return pltpu.make_async_copy(tensor_ref.at[k], slab.at[k], load_sem.at[k])

    for k in range(hours):
        load(k).start()

    lane = lax.broadcasted_iota(jnp.int32, (half, 128), 1)
    low_lane = lane < 64
    tile = 512

    def project(k):
        for i in range(0, n_i, tile):
            block = dot16(factor[...], slab[k, i : i + tile, :], NT)
            for m in range(tile // 128):
                top, low = block[:half, m * 128 : (m + 1) * 128], block[half:, m * 128 : (m + 1) * 128]
                b = 2 * (i // 128 + m)
                rs1_send[k, b] = jnp.where(low_lane, top, pltpu.roll(low, 64, 1)).astype(rs1_send.dtype)
                rs1_send[k, b + 1] = jnp.where(low_lane, pltpu.roll(top, 64, 1), low).astype(rs1_send.dtype)
        rs1_recv[k, bld] = rs1_send[k, bld]
        start_exchange("bld", lambda peer: rs1_send.at[k, peer], rs1_recv.at[k, bld], lambda step: RS1 + k)

    def build_gram_start(gram):
        message = pack(gram)
        gb_send[...] = message
        gb_recv[bld] = message
        start_exchange("bld", lambda peer: gb_send, gb_recv.at[bld], lambda step: GB)

    def build_gram_finish():
        finish_exchange(GB, gb_recv.at[pl.ds(0, n_bld - 1)])
        total = gb_recv[0]
        for b in range(1, n_bld):
            total = total + gb_recv[b]
        return unpack(total)

    pad = hour_rows.shape[0]
    rows_k = lax.broadcasted_iota(jnp.int32, (pad, hours * 128), 0)
    lanes_k = lax.broadcasted_iota(jnp.int32, (pad, hours * 128), 1)
    pick = (rows_k == lanes_k // 128).astype(jnp.float32)

    hour_rows[...] = jnp.zeros_like(hour_rows)
    hour_rows[0:hours, :] = hour_ref[...] / scale_up
    hour_cols[...] = dot32(identity(rank), hour_rows[...], NT)
    inv_b_col[...] = jnp.ones_like(inv_b_col)
    start_factor = build_ref[...]
    factor[...] = start_factor.astype(jnp.bfloat16)
    gram0 = dot32(start_factor, start_factor, NT)

    pl.semaphore_wait(barrier, n_bld + n_smp - 2)
    build_gram_start(gram0)
    for k in range(hours):
        load(k).wait()
        project(k)
    gram_build[...] = build_gram_finish()

    @pl.loop(0, SWEEPS)
    def _(sweep):
        for k in range(hours):
            finish_exchange(RS1 + k, rs1_recv.at[k, pl.ds(0, n_bld - 1)])
        right = None
        for k in range(hours):
            col = hour_cols[:, k : k + 1] * inv_b_col[:, 0:1]
            both = jnp.where(
                low_lane,
                jnp.broadcast_to(col[:half], (half, 128)),
                jnp.broadcast_to(col[half:], (half, 128)),
            )
            total = rs1_recv[k, 0].astype(jnp.float32)
            for b in range(1, n_bld):
                total = total + rs1_recv[k, b].astype(jnp.float32)
            right = both * total if right is None else right + both * total
        s_slice[...] = right
        message = right.astype(jnp.bfloat16)
        ag1_send[...] = message
        ag1_recv[bld] = message
        start_exchange("bld", lambda peer: ag1_send, ag1_recv.at[bld], lambda step: AG1 + step[0])

        gram_hour = dot32(hour_cols[...], hour_rows[...])
        inverse = regularized_inverse(gram_build[...] * gram_hour)
        inv_sample[...] = inverse
        parts = three_parts(inverse)

        for order, dy in enumerate((0, 1, 3, 2)):
            chunk = (y - dy + 4) % 4
            first = chunk * 4
            finish_exchange(AG1 + dy, ag1_recv.at[pl.ds(0, 3 if dy == 0 else 4)])
            for m in range(2):
                even = ag1_recv[first + 2 * m].astype(jnp.float32)
                odd = ag1_recv[first + 2 * m + 1].astype(jnp.float32)
                top = jnp.where(low_lane, even, pltpu.roll(odd, 64, 1))
                low = jnp.where(low_lane, pltpu.roll(even, 64, 1), odd)
                columns = jnp.concatenate([top, low], axis=0).astype(jnp.bfloat16)
                solved = dot16(parts, columns)
                solved = solved[:rank] + (solved[rank : 2 * rank] + solved[2 * rank :])
                where = pl.multiple_of(chunk * 256 + m * 128, 128)
                factor[:, pl.ds(where, 128)] = solved.astype(jnp.bfloat16)
            rows = pl.ds(pl.multiple_of(chunk * 256, 256), 256)
            if order == 3:
                gram_part = pack(dot16(factor[...], factor[...], NT))
                gs_send[...] = gram_part
                gs_recv[smp] = gram_part
                start_exchange("smp", lambda peer: gs_send, gs_recv.at[smp], lambda step: GS)
            for k in range(hours):
                for j in range(0, n_j, tile):
                    block = dot16(factor[:, rows], slab[k, rows, j : j + tile])
                    if order == 0:
                        mixed[k, :, j : j + tile] = block
                    else:
                        mixed[k, :, j : j + tile] += block

        cols = [jnp.broadcast_to(hour_cols[:, k : k + 1], (rank, 128)) for k in range(hours)]
        for s in range(n_smp):
            block = cols[0] * mixed[0, :, s * 128 : (s + 1) * 128]
            for k in range(1, hours):
                block = block + cols[k] * mixed[k, :, s * 128 : (s + 1) * 128]
            rs2_send[s] = block.astype(rs2_send.dtype)
        rs2_recv[smp] = rs2_send[smp]
        start_exchange("smp", lambda peer: rs2_send.at[peer], rs2_recv.at[smp], lambda step: RS2)

        finish_exchange(GS, gs_recv.at[pl.ds(0, n_smp - 1)])
        gram_raw = gs_recv[0]
        for s in range(1, n_smp):
            gram_raw = gram_raw + gs_recv[s]
        gram_raw = unpack(gram_raw)
        inv_row, inv_col = scales_of(gram_raw, samples_total)
        inv_s_row[...] = jnp.broadcast_to(inv_row, inv_s_row.shape)
        inv_s_col[...] = jnp.broadcast_to(inv_col, inv_s_col.shape)
        gram_sample[...] = gram_raw * (inv_col * inv_row)
        inverse = regularized_inverse(gram_sample[...] * gram_hour) * inv_row

        finish_exchange(RS2, rs2_recv.at[pl.ds(0, n_smp - 1)])
        total = rs2_recv[0].astype(jnp.float32)
        for s in range(1, n_smp):
            total = total + rs2_recv[s].astype(jnp.float32)
        unscaled = dot32(inverse, total)
        ub_slice[...] = unscaled
        message = unscaled.astype(jnp.bfloat16)
        ag2_send[...] = message
        ag2_recv[smp] = message
        start_exchange("smp", lambda peer: ag2_send, ag2_recv.at[smp], lambda step: AG2)
        finish_exchange(AG2, ag2_recv.at[pl.ds(0, n_smp - 1)])

        sums = []
        for k in range(hours):
            acc = jnp.zeros((rank, 128), jnp.float32)
            for s in range(n_smp):
                acc = acc + mixed[k, :, s * 128 : (s + 1) * 128] * ag2_recv[s].astype(jnp.float32)
            sums.append(acc)
        hour_terms = dot32(pick, jnp.concatenate(sums, axis=1), NT)
        message = jnp.concatenate([hour_terms, jnp.zeros_like(hour_terms)], axis=1)
        p1_send[...] = message
        p1_recv[bld] = message
        start_exchange("bld", lambda peer: p1_send, p1_recv.at[bld], lambda step: P1)
        for s in range(n_smp):
            factor[:, s * 128 : (s + 1) * 128] = ag2_recv[s]
        build_gram_start(dot16(factor[...], factor[...], NT))

        @pl.when(sweep < SWEEPS - 1)
        def _():
            for k in range(hours):
                project(k)

        finish_exchange(P1, p1_recv.at[pl.ds(0, n_bld - 1)])
        total = p1_recv[0]
        for b in range(1, n_bld):
            total = total + p1_recv[b]
        p2_send[...] = total
        p2_recv[smp] = total
        start_exchange("smp", lambda peer: p2_send, p2_recv.at[smp], lambda step: P2)

        gram_raw = build_gram_finish()
        inv_row, inv_col = scales_of(gram_raw, buildings_total)
        inv_b_col[...] = jnp.broadcast_to(inv_col, inv_b_col.shape)
        gram_build[...] = gram_raw * (inv_col * inv_row)
        inverse = regularized_inverse(gram_sample[...] * gram_build[...])

        finish_exchange(P2, p2_recv.at[pl.ds(0, n_smp - 1)])
        hour_sum = p2_recv[0]
        for s in range(1, n_smp):
            hour_sum = hour_sum + p2_recv[s]
        hour_rhs = hour_sum[:, :rank] * (inv_row * inv_s_row[0:1, :])
        hour_cols[...] = dot32(inverse, hour_rhs, NT)
        hour_rows[...] = dot32(hour_rhs, inverse)

    sample_out[...] = dot32(inv_sample[...], unpack(s_slice[...])) * inv_s_col[:, 0:1]
    build_out[...] = ub_slice[...] * inv_b_col[:, 0:1]
    hour_out[...] = hour_rows[0:hours, :] * scale_up


def local(tensor, building_factor, hour_weights):
    n_smp = lax.axis_size("smp")
    n_bld = lax.axis_size("bld")
    hours, n_i, n_j = tensor.shape
    rank = building_factor.shape[0]
    assert (n_smp, n_bld, rank, hours) == (8, 16, 64, 4)
    i_share, j_share = n_i // n_bld, n_j // n_smp
    assert (i_share, j_share) == (64, 128)
    f32, bf16 = jnp.float32, jnp.bfloat16
    body = functools.partial(kernel, n_smp, n_bld, n_i * n_smp, n_j * n_bld)
    vmem = pl.BlockSpec(memory_space=pltpu.VMEM)
    pad = 8
    return pl.pallas_call(
        body,
        out_shape=(
            jax.ShapeDtypeStruct((rank, i_share), f32),
            jax.ShapeDtypeStruct((rank, j_share), f32),
            jax.ShapeDtypeStruct((hours, rank), f32),
        ),
        in_specs=[pl.BlockSpec(memory_space=pl.ANY), vmem, vmem],
        out_specs=(vmem, vmem, vmem),
        scratch_shapes=[
            pltpu.VMEM((hours, n_i, n_j), bf16),
            pltpu.VMEM((hours, rank, n_j), f32),
            pltpu.VMEM((rank, n_j), bf16),
            pltpu.VMEM((rank // 2, 2 * i_share), f32),
            pltpu.VMEM((rank, j_share), f32),
            pltpu.VMEM((rank, rank), f32),
            pltpu.VMEM((rank, rank), f32),
            pltpu.VMEM((rank, rank), f32),
            pltpu.VMEM((pad, rank), f32),
            pltpu.VMEM((rank, pad), f32),
            pltpu.VMEM((rank, pad), f32),
            pltpu.VMEM((pad, rank), f32),
            pltpu.VMEM((rank, pad), f32),
            pltpu.VMEM((hours, n_bld, rank // 2, 2 * i_share), bf16),
            pltpu.VMEM((hours, n_bld, rank // 2, 2 * i_share), bf16),
            pltpu.VMEM((rank // 2, 2 * i_share), bf16),
            pltpu.VMEM((n_bld, rank // 2, 2 * i_share), bf16),
            pltpu.VMEM((rank // 2, 2 * rank), f32),
            pltpu.VMEM((n_smp, rank // 2, 2 * rank), f32),
            pltpu.VMEM((n_smp, rank, j_share), bf16),
            pltpu.VMEM((n_smp, rank, j_share), bf16),
            pltpu.VMEM((rank, j_share), bf16),
            pltpu.VMEM((n_smp, rank, j_share), bf16),
            pltpu.VMEM((rank // 2, 2 * rank), f32),
            pltpu.VMEM((n_bld, rank // 2, 2 * rank), f32),
            pltpu.VMEM((pad, 2 * rank), f32),
            pltpu.VMEM((n_bld, pad, 2 * rank), f32),
            pltpu.VMEM((pad, 2 * rank), f32),
            pltpu.VMEM((n_smp, pad, 2 * rank), f32),
            pltpu.SemaphoreType.DMA((hours,)),
            pltpu.SemaphoreType.DMA((COUNT,)),
            pltpu.SemaphoreType.DMA((COUNT,)),
        ],
        compiler_params=pltpu.CompilerParams(
            collective_id=0, has_side_effects=True, vmem_limit_bytes=40 * 1024 * 1024
        ),
        name="als_sweeps",
    )(tensor, building_factor, hour_weights)


def solution(mesh):
    in_specs = (P(None, "smp", "bld"), P(None, "bld"), P())
    out_specs = (P(None, ("smp", "bld")), P(None, ("bld", "smp")), P())
    return jax.shard_map(local, mesh=mesh, in_specs=in_specs, out_specs=out_specs, check_vma=False)
```

```python
import functools
import math

import jax
import jax.numpy as jnp
from jax import lax
from jax.experimental import pallas as pl
from jax.experimental.pallas import tpu as pltpu
from jax.sharding import PartitionSpec as P

SWEEPS = 5
EPSILON = 1e-06
RIDGE_SHARE = 0.05
HIGHEST = lax.Precision.HIGHEST
MESH = pl.DeviceIdType.MESH
NT = (((1,), (1,)), ((), ()))
NN = (((1,), (0,)), ((), ()))

BLD_STEPS = [
    (dy, dx, dc) for dy in (2, 1, 3, 0) for dx in (1, 0) for dc in (1, 0) if (dy, dx, dc) != (0, 0, 0)
]
SMP_STEPS = [(dx, dz) for dz in (2, 1, 3, 0) for dx in (1, 0) if (dx, dz) != (0, 0)]


def dot32(a, b, dims=NN):
    return lax.dot_general(a, b, dims, precision=HIGHEST, preferred_element_type=jnp.float32)


def dot16(a, b, dims=NN):
    return lax.dot_general(a, b, dims, preferred_element_type=jnp.float32)


def identity(n):
    rows = lax.broadcasted_iota(jnp.int32, (n, n), 0)
    cols = lax.broadcasted_iota(jnp.int32, (n, n), 1)
    return (rows == cols).astype(jnp.float32)


def pack(square):
    half = square.shape[0] // 2
    return jnp.concatenate([square[:half], square[half:]], axis=1)


def low_lanes(rows):
    return lax.broadcasted_iota(jnp.int32, (rows, 128), 1) < 64


def unpack_twice(packed):
    turned = pltpu.roll(packed, 64, 1)
    low = low_lanes(packed.shape[0])
    return jnp.concatenate([jnp.where(low, packed, turned), jnp.where(low, turned, packed)], axis=0)


def identity_twice(n):
    rows = lax.broadcasted_iota(jnp.int32, (n, 2 * n), 0)
    cols = lax.broadcasted_iota(jnp.int32, (n, 2 * n), 1)
    return ((cols == rows) | (cols == rows + n)).astype(jnp.float32)


def split(x):
    high = x.astype(jnp.bfloat16).astype(jnp.float32)
    rest = x - high
    middle = rest.astype(jnp.bfloat16).astype(jnp.float32)
    return high, middle, rest - middle


def low16(*arrays):
    return [array.astype(jnp.bfloat16) for array in arrays]


def left_parts(a):
    high, middle, rest = split(a)
    low = low_lanes(a.shape[0])
    one = jnp.concatenate(low16(high, jnp.where(low, middle, high)), axis=1)
    two = jnp.where(low, rest, middle).astype(jnp.bfloat16)
    return one, two


def product(a, b):
    one, two = left_parts(a)
    high, middle, rest = low16(*split(b))
    return dot16(one, jnp.concatenate([high, middle, high, rest], axis=0)) + dot16(
        two, jnp.concatenate([high, middle], axis=0)
    )


def product_two_parts(a, b):
    high, middle, _ = low16(*split(a))
    over, under, _ = low16(*split(b))
    return dot16(
        jnp.concatenate([high, middle], axis=1), jnp.concatenate([over, under, over, under], axis=0)
    )


def regularized_inverse(gram):
    n = gram.shape[0]
    eye = identity_twice(n)
    mean = jnp.sum(jnp.sum(gram * eye, axis=0, keepdims=True), axis=1, keepdims=True) / (2 * n)
    scale = 2.0 / ((n + 2 * RIDGE_SHARE) * mean)
    t = scale * (gram + RIDGE_SHARE * mean * eye)
    y = None
    spread = n / (n + 2 * RIDGE_SHARE)
    steps = 8
    for step in range(steps):
        spread = spread * spread / (2.0 - spread * spread)
        gain = 1.0 + spread
        factor = gain * (2.0 * eye - t)
        if step == 0:
            y = factor
            t = product(t, factor)
        elif step < steps - 1:
            both = product(jnp.concatenate([y, t], axis=0), factor)
            y, t = both[:n], both[n:]
        else:
            y = product(y, factor)
    return scale * y


def scales_of(gram_raw, count):
    n = gram_raw.shape[0]
    diagonal = gram_raw * identity_twice(n)
    inv_row = 1.0 / jnp.sqrt(jnp.sum(diagonal, axis=0, keepdims=True) / count + EPSILON)
    inv_col = 1.0 / jnp.sqrt(jnp.sum(diagonal, axis=1, keepdims=True) / (2 * count) + EPSILON)
    return inv_row, inv_col


RS1, AG1, GS, RS2, AG2, GB, P1, P2, GB0, COUNT = 0, 4, 8, 9, 10, 11, 12, 13, 14, 15


def kernel(
    n_smp, n_bld, samples_total, buildings_total,
    tensor_ref, build_ref, hour_ref,
    sample_out, build_out, hour_out,
    slab, mixed, factor, s_slice, ub_slice,
    gram_build, gram_sample, inv_sample, inv_hour, hour_rhs, hour_cols, inv_b_col, inv_s_row, inv_s_col,
    rs1_send, rs1_recv, ag1_send, ag1_recv, gs_send, gs_recv,
    rs2_send, rs2_recv, ag2_send, ag2_recv, gb_send, gb_recv, gb0_send, gb0_recv, p1_send, p1_recv, p2_send, p2_recv,
    load_sem, send_sems, recv_sems,
):
    hours, n_i, n_j = slab.shape
    rank = build_ref.shape[0]
    half = rank // 2
    scale_up = math.sqrt(samples_total * buildings_total)
    smp = lax.axis_index("smp")
    bld = lax.axis_index("bld")
    core = bld % 2
    x_hi = (bld // 2) % 2
    y = bld // 4
    z = smp % 4
    x_lo = smp // 4

    def bld_peer(step):
        dy, dx, dc = step
        return ((y + dy) % 4) * 4 + ((x_hi + dx) % 2) * 2 + (core + dc) % 2

    def smp_peer(step):
        dx, dz = step
        return ((x_lo + dx) % 2) * 4 + (z + dz) % 4

    bld_peers = [bld_peer(step) for step in BLD_STEPS]
    smp_peers = [smp_peer(step) for step in SMP_STEPS]

    def start_exchange(axis, piece_of, place, sem_of):
        peers, steps = (bld_peers, BLD_STEPS) if axis == "bld" else (smp_peers, SMP_STEPS)
        for peer, step in zip(peers, steps):
            pltpu.make_async_remote_copy(
                src_ref=piece_of(peer),
                dst_ref=place,
                send_sem=send_sems.at[sem_of(step)],
                recv_sem=recv_sems.at[sem_of(step)],
                device_id={axis: peer},
                device_id_type=MESH,
            ).start()

    def finish_exchange(sem, pieces):
        done = pltpu.make_async_remote_copy(
            src_ref=pieces,
            dst_ref=pieces,
            send_sem=send_sems.at[sem],
            recv_sem=recv_sems.at[sem],
            device_id={"bld": bld_peers[0]},
            device_id_type=MESH,
        )
        done.wait_recv()
        done.wait_send()

    barrier = pltpu.get_barrier_semaphore()
    for peer in bld_peers:
        pl.semaphore_signal(barrier, inc=1, device_id={"bld": peer}, device_id_type=MESH)
    for peer in smp_peers:
        pl.semaphore_signal(barrier, inc=1, device_id={"smp": peer}, device_id_type=MESH)

    def load(k):
        return pltpu.make_async_copy(tensor_ref.at[k], slab.at[k], load_sem.at[k])

    for k in range(hours):
        load(k).start()

    low_lane = low_lanes(half)
    tile = 512

    def project(k):
        for i in range(0, n_i, tile):
            block = dot16(factor[...], slab[k, i : i + tile, :], NT)
            for m in range(tile // 128):
                top, low = block[:half, m * 128 : (m + 1) * 128], block[half:, m * 128 : (m + 1) * 128]
                b = 2 * (i // 128 + m)
                rs1_send[k, b] = jnp.where(low_lane, top, pltpu.roll(low, 64, 1)).astype(rs1_send.dtype)
                rs1_send[k, b + 1] = jnp.where(low_lane, pltpu.roll(top, 64, 1), low).astype(rs1_send.dtype)
        rs1_recv[k, bld] = rs1_send[k, bld]
        start_exchange("bld", lambda peer: rs1_send.at[k, peer], rs1_recv.at[k, bld], lambda step: RS1 + k)

    def build_gram_start(gram, send, recv, sem):
        message = pack(gram)
        send[...] = message
        recv[bld] = message
        start_exchange("bld", lambda peer: send, recv.at[bld], lambda step: sem)

    def build_gram_finish(recv, sem):
        finish_exchange(sem, recv.at[pl.ds(0, n_bld - 1)])
        total = recv[0]
        for b in range(1, n_bld):
            total = total + recv[b]
        return unpack_twice(total)

    pad = hour_rhs.shape[0]
    pick_rows = lax.broadcasted_iota(jnp.int32, (pad, 128), 0)
    quarter = lax.broadcasted_iota(jnp.int32, (pad, 128), 1) // 32
    held = jnp.where(quarter == 0, 2, jnp.where(quarter == 1, 0, jnp.where(quarter == 2, 3, 1)))
    pick = (pick_rows == held).astype(jnp.bfloat16)

    def lane_sums(sums):
        low = low_lanes(rank)
        folded = [x + pltpu.roll(x, 64, 1) for x in sums]
        first = jnp.where(low, folded[0], folded[1])
        second = jnp.where(low, folded[2], folded[3])
        first = first + pltpu.roll(first, 32, 1)
        second = second + pltpu.roll(second, 96, 1)
        upper = (lax.broadcasted_iota(jnp.int32, (rank, 128), 1) // 32) % 2 == 1
        parts = low16(*split(jnp.where(upper, first, second)))
        rows = dot16(jnp.concatenate([pick] * 3, axis=1), jnp.concatenate(parts, axis=1), NT)
        return jnp.concatenate([rows, rows], axis=1)

    hour_rhs[...] = jnp.zeros_like(hour_rhs)
    hour_rhs[0:hours, 0:rank] = hour_ref[...] / scale_up
    inv_hour[...] = identity_twice(rank)
    hour_cols[...] = dot32(identity(rank), hour_rhs[:, 0:rank], NT)
    inv_b_col[...] = jnp.ones_like(inv_b_col)
    factor[...] = build_ref[...].astype(jnp.bfloat16)

    pl.semaphore_wait(barrier, n_bld + n_smp - 2)
    for k in range(hours):
        load(k).wait()
        project(k)
    build_gram_start(dot32(build_ref[...], build_ref[...], NT), gb0_send, gb0_recv, GB0)

    @pl.loop(0, SWEEPS)
    def _(sweep):
        for k in range(hours):
            finish_exchange(RS1 + k, rs1_recv.at[k, pl.ds(0, n_bld - 1)])
        right = None
        for k in range(hours):
            col = hour_cols[:, k : k + 1] * inv_b_col[:, 0:1]
            both = jnp.where(
                low_lane,
                jnp.broadcast_to(col[:half], (half, 128)),
                jnp.broadcast_to(col[half:], (half, 128)),
            )
            total = rs1_recv[k, 0].astype(jnp.float32)
            for b in range(1, n_bld):
                total = total + rs1_recv[k, b].astype(jnp.float32)
            right = both * total if right is None else right + both * total
        s_slice[...] = right
        message = right.astype(jnp.bfloat16)
        ag1_send[...] = message
        ag1_recv[bld] = message
        start_exchange("bld", lambda peer: ag1_send, ag1_recv.at[bld], lambda step: AG1 + step[0])

        @pl.when(sweep == 0)
        def _():
            gram_build[...] = build_gram_finish(gb0_recv, GB0)

        gram_hour = dot32(hour_cols[...], dot32(hour_rhs[:, 0:rank], inv_hour[...]))
        inverse = regularized_inverse(gram_build[...] * gram_hour)
        inv_sample[...] = inverse
        parts = jnp.concatenate(low16(*split(inverse)), axis=0)[:, :rank]
        gram_part = jnp.zeros((rank, rank), jnp.float32)

        for order, dy in enumerate((0, 1, 3, 2)):
            chunk = (y - dy + 4) % 4
            first = chunk * 4
            finish_exchange(AG1 + dy, ag1_recv.at[pl.ds(0, 3 if dy == 0 else 4)])
            columns = []
            for m in range(2):
                even = ag1_recv[first + 2 * m].astype(jnp.float32)
                odd = ag1_recv[first + 2 * m + 1].astype(jnp.float32)
                top = jnp.where(low_lane, even, pltpu.roll(odd, 64, 1))
                low = jnp.where(low_lane, pltpu.roll(even, 64, 1), odd)
                columns.append(jnp.concatenate([top, low], axis=0).astype(jnp.bfloat16))
            solved = dot16(parts, jnp.concatenate(columns, axis=1))
            solved = solved[:rank] + (solved[rank : 2 * rank] + solved[2 * rank :])
            solved = solved.astype(jnp.bfloat16)
            rows = pl.ds(pl.multiple_of(chunk * 256, 256), 256)
            gram_part = gram_part + dot16(solved, solved, NT)
            if order == 3:
                message = pack(gram_part)
                gs_send[...] = message
                gs_recv[smp] = message
                start_exchange("smp", lambda peer: gs_send, gs_recv.at[smp], lambda step: GS)
            for k in range(hours):
                for j in range(0, n_j, tile):
                    block = dot16(solved, slab[k, rows, j : j + tile])
                    if order == 0:
                        mixed[k, :, j : j + tile] = block
                    else:
                        mixed[k, :, j : j + tile] += block

        cols = [jnp.broadcast_to(hour_cols[:, k : k + 1], (rank, 128)) for k in range(hours)]
        for s in range(n_smp):
            block = cols[0] * mixed[0, :, s * 128 : (s + 1) * 128]
            for k in range(1, hours):
                block = block + cols[k] * mixed[k, :, s * 128 : (s + 1) * 128]
            rs2_send[s] = block.astype(rs2_send.dtype)
        rs2_recv[smp] = rs2_send[smp]
        start_exchange("smp", lambda peer: rs2_send.at[peer], rs2_recv.at[smp], lambda step: RS2)

        finish_exchange(GS, gs_recv.at[pl.ds(0, n_smp - 1)])
        gram_raw = gs_recv[0]
        for s in range(1, n_smp):
            gram_raw = gram_raw + gs_recv[s]
        gram_raw = unpack_twice(gram_raw)
        inv_row, inv_col = scales_of(gram_raw, samples_total)
        inv_s_row[...] = jnp.broadcast_to(inv_row, inv_s_row.shape)
        inv_s_col[...] = jnp.broadcast_to(inv_col, inv_s_col.shape)
        gram_sample[...] = gram_raw * (inv_col * inv_row)
        inverse = regularized_inverse(gram_sample[...] * gram_hour) * inv_row

        finish_exchange(RS2, rs2_recv.at[pl.ds(0, n_smp - 1)])
        total = rs2_recv[0].astype(jnp.float32)
        for s in range(1, n_smp):
            total = total + rs2_recv[s].astype(jnp.float32)
        unscaled = product_two_parts(inverse, total)
        ub_slice[...] = unscaled
        message = unscaled.astype(jnp.bfloat16)
        ag2_send[...] = message
        ag2_recv[smp] = message
        start_exchange("smp", lambda peer: ag2_send, ag2_recv.at[smp], lambda step: AG2)
        finish_exchange(AG2, ag2_recv.at[pl.ds(0, n_smp - 1)])

        sums = []
        for k in range(hours):
            acc = jnp.zeros((rank, 128), jnp.float32)
            for s in range(n_smp):
                acc = acc + mixed[k, :, s * 128 : (s + 1) * 128] * ag2_recv[s].astype(jnp.float32)
            sums.append(acc)
        message = lane_sums(sums)
        p1_send[...] = message
        p1_recv[bld] = message
        start_exchange("bld", lambda peer: p1_send, p1_recv.at[bld], lambda step: P1)
        for s in range(n_smp):
            factor[:, s * 128 : (s + 1) * 128] = ag2_recv[s]
        build_gram_start(dot16(factor[...], factor[...], NT), gb_send, gb_recv, GB)

        @pl.when(sweep < SWEEPS - 1)
        def _():
            for k in range(hours):
                project(k)

        finish_exchange(P1, p1_recv.at[pl.ds(0, n_bld - 1)])
        total = p1_recv[0]
        for b in range(1, n_bld):
            total = total + p1_recv[b]
        p2_send[...] = total
        p2_recv[smp] = total
        start_exchange("smp", lambda peer: p2_send, p2_recv.at[smp], lambda step: P2)

        gram_raw = build_gram_finish(gb_recv, GB)
        inv_row, inv_col = scales_of(gram_raw, buildings_total)
        inv_b_col[...] = jnp.broadcast_to(inv_col, inv_b_col.shape)
        gram_build[...] = gram_raw * (inv_col * inv_row)
        inverse = regularized_inverse(gram_sample[...] * gram_build[...])
        inv_hour[...] = inverse
        one, two = left_parts(inverse)
        scale_row = inv_row * inv_s_row[0:1, :]

        finish_exchange(P2, p2_recv.at[pl.ds(0, n_smp - 1)])
        total = p2_recv[0]
        for s in range(1, n_smp):
            total = total + p2_recv[s]
        right = total * scale_row
        hour_rhs[...] = right
        high, middle, rest = split(right)
        low = low_lanes(pad)
        both = jnp.where(low, high, middle).astype(jnp.bfloat16)
        far = jnp.where(low, high, rest).astype(jnp.bfloat16)
        hour_cols[...] = dot16(one, jnp.concatenate([both, far], axis=1), NT) + dot16(two, both, NT)

    sample_out[...] = product(inv_sample[...], unpack_twice(s_slice[...]))[:, :rank] * inv_s_col[:, 0:1]
    build_out[...] = ub_slice[...] * inv_b_col[:, 0:1]
    hour_out[...] = dot32(hour_rhs[:, 0:rank], inv_hour[:, 0:rank])[0:hours] * scale_up


def local(tensor, building_factor, hour_weights):
    n_smp = lax.axis_size("smp")
    n_bld = lax.axis_size("bld")
    hours, n_i, n_j = tensor.shape
    rank = building_factor.shape[0]
    assert (n_smp, n_bld, rank, hours) == (8, 16, 64, 4)
    i_share, j_share = n_i // n_bld, n_j // n_smp
    assert (i_share, j_share) == (64, 128)
    f32, bf16 = jnp.float32, jnp.bfloat16
    body = functools.partial(kernel, n_smp, n_bld, n_i * n_smp, n_j * n_bld)
    vmem = pl.BlockSpec(memory_space=pltpu.VMEM)
    pad = 8
    return pl.pallas_call(
        body,
        out_shape=(
            jax.ShapeDtypeStruct((rank, i_share), f32),
            jax.ShapeDtypeStruct((rank, j_share), f32),
            jax.ShapeDtypeStruct((hours, rank), f32),
        ),
        in_specs=[pl.BlockSpec(memory_space=pl.ANY), vmem, vmem],
        out_specs=(vmem, vmem, vmem),
        scratch_shapes=[
            pltpu.VMEM((hours, n_i, n_j), bf16),
            pltpu.VMEM((hours, rank, n_j), f32),
            pltpu.VMEM((rank, n_j), bf16),
            pltpu.VMEM((rank // 2, 2 * i_share), f32),
            pltpu.VMEM((rank, j_share), f32),
            pltpu.VMEM((rank, 2 * rank), f32),
            pltpu.VMEM((rank, 2 * rank), f32),
            pltpu.VMEM((rank, 2 * rank), f32),
            pltpu.VMEM((rank, 2 * rank), f32),
            pltpu.VMEM((pad, 2 * rank), f32),
            pltpu.VMEM((rank, pad), f32),
            pltpu.VMEM((rank, pad), f32),
            pltpu.VMEM((pad, 2 * rank), f32),
            pltpu.VMEM((rank, pad), f32),
            pltpu.VMEM((hours, n_bld, rank // 2, 2 * i_share), bf16),
            pltpu.VMEM((hours, n_bld, rank // 2, 2 * i_share), bf16),
            pltpu.VMEM((rank // 2, 2 * i_share), bf16),
            pltpu.VMEM((n_bld, rank // 2, 2 * i_share), bf16),
            pltpu.VMEM((rank // 2, 2 * rank), f32),
            pltpu.VMEM((n_smp, rank // 2, 2 * rank), f32),
            pltpu.VMEM((n_smp, rank, j_share), bf16),
            pltpu.VMEM((n_smp, rank, j_share), bf16),
            pltpu.VMEM((rank, j_share), bf16),
            pltpu.VMEM((n_smp, rank, j_share), bf16),
            pltpu.VMEM((rank // 2, 2 * rank), f32),
            pltpu.VMEM((n_bld, rank // 2, 2 * rank), f32),
            pltpu.VMEM((rank // 2, 2 * rank), f32),
            pltpu.VMEM((n_bld, rank // 2, 2 * rank), f32),
            pltpu.VMEM((pad, 2 * rank), f32),
            pltpu.VMEM((n_bld, pad, 2 * rank), f32),
            pltpu.VMEM((pad, 2 * rank), f32),
            pltpu.VMEM((n_smp, pad, 2 * rank), f32),
            pltpu.SemaphoreType.DMA((hours,)),
            pltpu.SemaphoreType.DMA((COUNT,)),
            pltpu.SemaphoreType.DMA((COUNT,)),
        ],
        compiler_params=pltpu.CompilerParams(
            collective_id=0, has_side_effects=True, vmem_limit_bytes=60 * 1024 * 1024
        ),
        name="als_sweeps",
    )(tensor, building_factor, hour_weights)


def solution(mesh):
    in_specs = (P(None, "smp", "bld"), P(None, "bld"), P())
    out_specs = (P(None, ("smp", "bld")), P(None, ("bld", "smp")), P())
    return jax.shard_map(local, mesh=mesh, in_specs=in_specs, out_specs=out_specs, check_vma=False)
```

```python
import functools
import math

import jax
import jax.numpy as jnp
from jax import lax
from jax.experimental import pallas as pl
from jax.experimental.pallas import tpu as pltpu
from jax.sharding import PartitionSpec as P

SWEEPS = 5
EPSILON = 1e-06
RIDGE_SHARE = 0.05
HIGHEST = lax.Precision.HIGHEST
MESH = pl.DeviceIdType.MESH
NT = (((1,), (1,)), ((), ()))
NN = (((1,), (0,)), ((), ()))

BLD_STEPS = [
    (dy, dx, dc) for dy in (2, 1, 3, 0) for dx in (1, 0) for dc in (1, 0) if (dy, dx, dc) != (0, 0, 0)
]
SMP_STEPS = [(dx, dz) for dz in (2, 1, 3, 0) for dx in (1, 0) if (dx, dz) != (0, 0)]


def dot32(a, b, dims=NN):
    return lax.dot_general(a, b, dims, precision=HIGHEST, preferred_element_type=jnp.float32)


def dot16(a, b, dims=NN):
    return lax.dot_general(a, b, dims, preferred_element_type=jnp.float32)


def identity(n):
    rows = lax.broadcasted_iota(jnp.int32, (n, n), 0)
    cols = lax.broadcasted_iota(jnp.int32, (n, n), 1)
    return (rows == cols).astype(jnp.float32)


def pack(square):
    half = square.shape[0] // 2
    return jnp.concatenate([square[:half], square[half:]], axis=1)


def low_lanes(rows):
    return lax.broadcasted_iota(jnp.int32, (rows, 128), 1) < 64


def unpack_twice(packed):
    turned = pltpu.roll(packed, 64, 1)
    low = low_lanes(packed.shape[0])
    return jnp.concatenate([jnp.where(low, packed, turned), jnp.where(low, turned, packed)], axis=0)


def identity_twice(n):
    rows = lax.broadcasted_iota(jnp.int32, (n, 2 * n), 0)
    cols = lax.broadcasted_iota(jnp.int32, (n, 2 * n), 1)
    return ((cols == rows) | (cols == rows + n)).astype(jnp.float32)


def split(x):
    high = x.astype(jnp.bfloat16).astype(jnp.float32)
    rest = x - high
    middle = rest.astype(jnp.bfloat16).astype(jnp.float32)
    return high, middle, rest - middle


def low16(*arrays):
    return [array.astype(jnp.bfloat16) for array in arrays]


def left_parts(a):
    high, middle, rest = split(a)
    low = low_lanes(a.shape[0])
    one = jnp.concatenate(low16(high, jnp.where(low, middle, high)), axis=1)
    two = jnp.where(low, rest, middle).astype(jnp.bfloat16)
    return one, two


def product(a, b):
    one, two = left_parts(a)
    high, middle, rest = low16(*split(b))
    return dot16(one, jnp.concatenate([high, middle, high, rest], axis=0)) + dot16(
        two, jnp.concatenate([high, middle], axis=0)
    )


def product_two_parts(a, b):
    high, middle, _ = low16(*split(a))
    over, under, _ = low16(*split(b))
    return dot16(
        jnp.concatenate([high, middle], axis=1), jnp.concatenate([over, under, over, under], axis=0)
    )


def regularized_inverse(gram):
    n = gram.shape[0]
    eye = identity_twice(n)
    mean = jnp.sum(jnp.sum(gram * eye, axis=0, keepdims=True), axis=1, keepdims=True) / (2 * n)
    scale = 2.0 / ((n + 2 * RIDGE_SHARE) * mean)
    t = scale * (gram + RIDGE_SHARE * mean * eye)
    y = None
    spread = n / (n + 2 * RIDGE_SHARE)
    steps = 8
    for step in range(steps):
        spread = spread * spread / (2.0 - spread * spread)
        gain = 1.0 + spread
        factor = gain * (2.0 * eye - t)
        if step == 0:
            y = factor
            t = product(t, factor)
        elif step < steps - 1:
            both = product(jnp.concatenate([y, t], axis=0), factor)
            y, t = both[:n], both[n:]
        else:
            y = product(y, factor)
    return scale * y


def scales_of(gram_raw, count):
    n = gram_raw.shape[0]
    diagonal = gram_raw * identity_twice(n)
    inv_row = 1.0 / jnp.sqrt(jnp.sum(diagonal, axis=0, keepdims=True) / count + EPSILON)
    inv_col = 1.0 / jnp.sqrt(jnp.sum(diagonal, axis=1, keepdims=True) / (2 * count) + EPSILON)
    return inv_row, inv_col


RS1, AG1, AG2, PAIR, GS, RS2, GB, P1, P2, GB0, GP, COUNT = 0, 4, 8, 12, 16, 17, 18, 19, 20, 21, 22, 23


def kernel(
    n_smp, n_bld, samples_total, buildings_total,
    tensor_ref, build_ref, hour_ref,
    sample_out, build_out, hour_out,
    slab, mixed, partial, own, pair_send, pair_recv, gp_send, gp_recv, s_slice, ub_slice,
    gram_build, gram_sample, inv_sample, inv_hour, hour_rhs, hour_cols, inv_b_col, inv_s_row, inv_s_col,
    rs1_send, rs1_recv, ag1_send, ag1_recv, gs_send, gs_recv,
    rs2_send, rs2_recv, ag2_send, ag2_recv, gb_send, gb_recv, gb0_send, gb0_recv, p1_send, p1_recv, p2_send, p2_recv,
    load_sem, send_sems, recv_sems,
):
    hours, n_i, n_j = slab.shape
    rank = build_ref.shape[0]
    half = rank // 2
    scale_up = math.sqrt(samples_total * buildings_total)
    smp = lax.axis_index("smp")
    bld = lax.axis_index("bld")
    core = bld % 2
    x_hi = (bld // 2) % 2
    y = bld // 4
    z = smp % 4
    x_lo = smp // 4

    def bld_peer(step):
        dy, dx, dc = step
        return ((y + dy) % 4) * 4 + ((x_hi + dx) % 2) * 2 + (core + dc) % 2

    def smp_peer(step):
        dx, dz = step
        return ((x_lo + dx) % 2) * 4 + (z + dz) % 4

    bld_peers = [bld_peer(step) for step in BLD_STEPS]
    like_steps = [step for step in BLD_STEPS if step[2] == 0]
    like_peers = [bld_peer(step) for step in like_steps]
    partner = bld_peer((0, 0, 1))
    chip = bld // 2
    n_chip = n_bld // 2
    smp_peers = [smp_peer(step) for step in SMP_STEPS]

    def start_exchange(axis, piece_of, place, sem_of):
        if axis == "like":
            peers, steps, axis = like_peers, like_steps, "bld"
        elif axis == "partner":
            peers, steps, axis = [partner], [(0, 0, 1)], "bld"
        elif axis == "bld":
            peers, steps = bld_peers, BLD_STEPS
        else:
            peers, steps = smp_peers, SMP_STEPS
        for peer, step in zip(peers, steps):
            pltpu.make_async_remote_copy(
                src_ref=piece_of(peer),
                dst_ref=place,
                send_sem=send_sems.at[sem_of(step)],
                recv_sem=recv_sems.at[sem_of(step)],
                device_id={axis: peer},
                device_id_type=MESH,
            ).start()

    def finish_exchange(sem, pieces):
        done = pltpu.make_async_remote_copy(
            src_ref=pieces,
            dst_ref=pieces,
            send_sem=send_sems.at[sem],
            recv_sem=recv_sems.at[sem],
            device_id={"bld": bld_peers[0]},
            device_id_type=MESH,
        )
        done.wait_recv()
        done.wait_send()

    barrier = pltpu.get_barrier_semaphore()
    for peer in bld_peers:
        pl.semaphore_signal(barrier, inc=1, device_id={"bld": peer}, device_id_type=MESH)
    for peer in smp_peers:
        pl.semaphore_signal(barrier, inc=1, device_id={"smp": peer}, device_id_type=MESH)

    def load(k):
        return pltpu.make_async_copy(tensor_ref.at[k], slab.at[k], load_sem.at[k])

    for k in range(hours):
        load(k).start()

    low_lane = low_lanes(half)
    tile = 512

    def scatter(k, i, block):
        for m in range(tile // 128):
            top, low = block[:half, m * 128 : (m + 1) * 128], block[half:, m * 128 : (m + 1) * 128]
            moved = pltpu.roll(jnp.where(low_lane, low, top), 64, 1)
            even = jnp.where(low_lane, top, moved)
            odd = jnp.where(low_lane, moved, low)
            own[k, i // 128 + m] = jnp.where(core == 0, even, odd)
            pair_send[k, i // 128 + m] = jnp.where(core == 0, odd, even).astype(pair_send.dtype)

    def pair_start(k):
        start_exchange("partner", lambda peer: pair_send.at[k], pair_recv.at[k], lambda step: PAIR + k)

    def pair_finish(k):
        finish_exchange(PAIR + k, pair_recv.at[k])
        for c in range(n_chip):
            rs1_send[k, c] = (own[k, c] + pair_recv[k, c].astype(jnp.float32)).astype(rs1_send.dtype)
        rs1_recv[k, chip] = rs1_send[k, chip]
        start_exchange("like", lambda peer: rs1_send.at[k, peer // 2], rs1_recv.at[k, chip], lambda step: RS1 + k)

    def slices(ref, index, groups):
        parts = []
        for group in groups:
            for first in (0, 4):
                parts.append(ref[index + (pl.ds(pl.multiple_of((first + group) * 128, 128), 128),)])
        return jnp.concatenate(parts, axis=-1)

    def gathered(groups):
        parts = []
        for group in groups:
            parts += [ag2_recv[group], ag2_recv[4 + group]]
        return jnp.concatenate(parts, axis=1)

    def project(k, i, groups):
        return dot16(gathered(groups), slices(slab, (k, slice(i, i + tile)), groups), NT)

    def build_gram_start(gram, send, recv, sem):
        message = pack(gram)
        send[...] = message
        recv[bld] = message
        start_exchange("bld", lambda peer: send, recv.at[bld], lambda step: sem)

    def build_gram_finish(recv, sem):
        others = recv.shape[0] - 1
        finish_exchange(sem, recv.at[pl.ds(0, others)])
        total = recv[0]
        for b in range(1, others + 1):
            total = total + recv[b]
        return unpack_twice(total)

    pad = hour_rhs.shape[0]
    pick_rows = lax.broadcasted_iota(jnp.int32, (pad, 128), 0)
    quarter = lax.broadcasted_iota(jnp.int32, (pad, 128), 1) // 32
    held = jnp.where(quarter == 0, 2, jnp.where(quarter == 1, 0, jnp.where(quarter == 2, 3, 1)))
    pick = (pick_rows == held).astype(jnp.bfloat16)

    def lane_sums(sums):
        low = low_lanes(rank)
        folded = [x + pltpu.roll(x, 64, 1) for x in sums]
        first = jnp.where(low, folded[0], folded[1])
        second = jnp.where(low, folded[2], folded[3])
        first = first + pltpu.roll(first, 32, 1)
        second = second + pltpu.roll(second, 96, 1)
        upper = (lax.broadcasted_iota(jnp.int32, (rank, 128), 1) // 32) % 2 == 1
        parts = low16(*split(jnp.where(upper, first, second)))
        rows = dot16(jnp.concatenate([pick] * 3, axis=1), jnp.concatenate(parts, axis=1), NT)
        return jnp.concatenate([rows, rows], axis=1)

    hour_rhs[...] = jnp.zeros_like(hour_rhs)
    hour_rhs[0:hours, 0:rank] = hour_ref[...] / scale_up
    inv_hour[...] = identity_twice(rank)
    hour_cols[...] = dot32(identity(rank), hour_rhs[:, 0:rank], NT)
    inv_b_col[...] = jnp.ones_like(inv_b_col)
    start_factor = build_ref[...].astype(jnp.bfloat16)
    for k in range(hours):
        load(k).wait()
        for i in range(0, n_i, tile):
            scatter(k, i, dot16(start_factor, slab[k, i : i + tile, :], NT))
        if k == 1:
            pl.semaphore_wait(barrier, n_bld + n_smp - 2)
            pair_start(0)
        if k >= 1:
            pair_start(k)
            pair_finish(k - 1)
    pair_finish(hours - 1)
    build_gram_start(dot32(build_ref[...], build_ref[...], NT), gb0_send, gb0_recv, GB0)

    @pl.loop(0, SWEEPS)
    def _(sweep):
        for k in range(hours):
            finish_exchange(RS1 + k, rs1_recv.at[k, pl.ds(0, n_chip - 1)])
        right = None
        for k in range(hours):
            col = hour_cols[:, k : k + 1] * inv_b_col[:, 0:1]
            both = jnp.where(
                low_lane,
                jnp.broadcast_to(col[:half], (half, 128)),
                jnp.broadcast_to(col[half:], (half, 128)),
            )
            total = rs1_recv[k, 0].astype(jnp.float32)
            for c in range(1, n_chip):
                total = total + rs1_recv[k, c].astype(jnp.float32)
            right = both * total if right is None else right + both * total
        s_slice[...] = right
        message = right.astype(jnp.bfloat16)
        ag1_send[...] = message
        ag1_recv[bld] = message
        start_exchange("bld", lambda peer: ag1_send, ag1_recv.at[bld], lambda step: AG1 + step[0])

        @pl.when(sweep == 0)
        def _():
            gram_build[...] = build_gram_finish(gb0_recv, GB0)

        gram_hour = dot32(hour_cols[...], dot32(hour_rhs[:, 0:rank], inv_hour[...]))
        inverse = regularized_inverse(gram_build[...] * gram_hour)
        inv_sample[...] = inverse
        parts = jnp.concatenate(low16(*split(inverse)), axis=0)[:, :rank]
        gram_part = jnp.zeros((rank, rank), jnp.float32)

        for order, dy in enumerate((0, 1, 3, 2)):
            chunk = (y - dy + 4) % 4
            first = chunk * 4
            finish_exchange(AG1 + dy, ag1_recv.at[pl.ds(0, 3 if dy == 0 else 4)])
            columns = []
            for m in range(2):
                even = ag1_recv[first + 2 * m].astype(jnp.float32)
                odd = ag1_recv[first + 2 * m + 1].astype(jnp.float32)
                moved = pltpu.roll(jnp.where(low_lane, odd, even), 64, 1)
                top = jnp.where(low_lane, even, moved)
                low = jnp.where(low_lane, moved, odd)
                columns.append(jnp.concatenate([top, low], axis=0).astype(jnp.bfloat16))
            solved = dot16(parts, jnp.concatenate(columns, axis=1))
            solved = solved[:rank] + (solved[rank : 2 * rank] + solved[2 * rank :])
            solved = solved.astype(jnp.bfloat16)
            rows = pl.ds(pl.multiple_of(chunk * 256, 256), 256)
            gram_part = gram_part + dot16(solved, solved, NT)
            if order == 3:
                message = pack(gram_part)
                gs_send[...] = message
                gs_recv[smp] = message
                start_exchange("smp", lambda peer: gs_send, gs_recv.at[smp], lambda step: GS)
            for k in range(hours):
                for j in range(0, n_j, tile):
                    block = dot16(solved, slab[k, rows, j : j + tile])
                    if order == 0:
                        mixed[k, :, j : j + tile] = block
                    else:
                        mixed[k, :, j : j + tile] += block

        cols = [jnp.broadcast_to(hour_cols[:, k : k + 1], (rank, 128)) for k in range(hours)]
        for s in range(n_smp):
            block = cols[0] * mixed[0, :, s * 128 : (s + 1) * 128]
            for k in range(1, hours):
                block = block + cols[k] * mixed[k, :, s * 128 : (s + 1) * 128]
            rs2_send[s] = block.astype(rs2_send.dtype)
        rs2_recv[smp] = rs2_send[smp]
        start_exchange("smp", lambda peer: rs2_send.at[peer], rs2_recv.at[smp], lambda step: RS2)

        finish_exchange(GS, gs_recv.at[pl.ds(0, n_smp - 1)])
        gram_raw = gs_recv[0]
        for s in range(1, n_smp):
            gram_raw = gram_raw + gs_recv[s]
        gram_raw = unpack_twice(gram_raw)
        inv_row, inv_col = scales_of(gram_raw, samples_total)
        inv_s_row[...] = jnp.broadcast_to(inv_row, inv_s_row.shape)
        inv_s_col[...] = jnp.broadcast_to(inv_col, inv_s_col.shape)
        gram_sample[...] = gram_raw * (inv_col * inv_row)
        inverse = regularized_inverse(gram_sample[...] * gram_hour) * inv_row

        finish_exchange(RS2, rs2_recv.at[pl.ds(0, n_smp - 1)])
        total = rs2_recv[0].astype(jnp.float32)
        for s in range(1, n_smp):
            total = total + rs2_recv[s].astype(jnp.float32)
        unscaled = product_two_parts(inverse, total)
        ub_slice[...] = unscaled
        message = unscaled.astype(jnp.bfloat16)
        ag2_send[...] = message
        ag2_recv[smp] = message
        start_exchange("smp", lambda peer: ag2_send, ag2_recv.at[smp], lambda step: AG2 + step[1])

        sums = [jnp.zeros((rank, 128), jnp.float32) for _ in range(hours)]
        gram_part = jnp.zeros((rank, rank), jnp.float32)
        before_last = sweep < SWEEPS - 1
        groups = [(z - dz + 4) % 4 for dz in (0, 1, 3, 2)]
        early = {k: groups[:2] if k < 2 else groups[:1] for k in range(hours)}
        for order, dz in enumerate((0, 1, 3, 2)):
            finish_exchange(AG2 + dz, ag2_recv.at[pl.ds(0, 1 if dz == 0 else 2)])
            group = groups[order]
            solved = gathered([group])
            gram_part = gram_part + dot16(solved, solved, NT)
            wide = solved.astype(jnp.float32)
            for k in range(hours):
                terms = slices(mixed, (k, slice(None)), [group]) * wide
                sums[k] = sums[k] + (terms[:, :128] + terms[:, 128:])
            if order < 2:

                @pl.when(before_last)
                def _():
                    for k in range(hours):
                        if order < len(early[k]):
                            for i in range(0, n_i, tile):
                                block = project(k, i, [group])
                                if order == 0:
                                    partial[k, :, i : i + tile] = block
                                else:
                                    partial[k, :, i : i + tile] += block

        message = lane_sums(sums)
        p1_send[...] = message
        p1_recv[bld] = message
        start_exchange("bld", lambda peer: p1_send, p1_recv.at[bld], lambda step: P1)
        message = pack(gram_part)
        gp_send[...] = message
        start_exchange("partner", lambda peer: gp_send, gp_recv, lambda step: GP)

        def finish_project(k):
            left = groups[len(early[k]) :]
            for i in range(0, n_i, tile):
                scatter(k, i, partial[k, :, i : i + tile] + project(k, i, left))
            pair_start(k)

        @pl.when(before_last)
        def _():
            finish_project(0)

        finish_exchange(GP, gp_recv)
        message = gp_send[...] + gp_recv[...]
        gb_send[...] = message
        gb_recv[chip] = message
        start_exchange("like", lambda peer: gb_send, gb_recv.at[chip], lambda step: GB)

        @pl.when(before_last)
        def _():
            for k in range(1, hours):
                finish_project(k)
                pair_finish(k - 1)
            pair_finish(hours - 1)

        finish_exchange(P1, p1_recv.at[pl.ds(0, n_bld - 1)])
        total = p1_recv[0]
        for b in range(1, n_bld):
            total = total + p1_recv[b]
        p2_send[...] = total
        p2_recv[smp] = total
        start_exchange("smp", lambda peer: p2_send, p2_recv.at[smp], lambda step: P2)

        gram_raw = build_gram_finish(gb_recv, GB)
        inv_row, inv_col = scales_of(gram_raw, buildings_total)
        inv_b_col[...] = jnp.broadcast_to(inv_col, inv_b_col.shape)
        gram_build[...] = gram_raw * (inv_col * inv_row)
        inverse = regularized_inverse(gram_sample[...] * gram_build[...])
        inv_hour[...] = inverse
        one, two = left_parts(inverse)
        scale_row = inv_row * inv_s_row[0:1, :]

        finish_exchange(P2, p2_recv.at[pl.ds(0, n_smp - 1)])
        total = p2_recv[0]
        for s in range(1, n_smp):
            total = total + p2_recv[s]
        right = total * scale_row
        hour_rhs[...] = right
        high, middle, rest = split(right)
        low = low_lanes(pad)
        both = jnp.where(low, high, middle).astype(jnp.bfloat16)
        far = jnp.where(low, high, rest).astype(jnp.bfloat16)
        hour_cols[...] = dot16(one, jnp.concatenate([both, far], axis=1), NT) + dot16(two, both, NT)

    sample_out[...] = product(inv_sample[...], unpack_twice(s_slice[...]))[:, :rank] * inv_s_col[:, 0:1]
    build_out[...] = ub_slice[...] * inv_b_col[:, 0:1]
    hour_out[...] = dot32(hour_rhs[:, 0:rank], inv_hour[:, 0:rank])[0:hours] * scale_up


def put_out(a_ref, b_ref, c_ref, a_out, b_out, c_out, sems):
    pairs = ((a_ref, a_out), (b_ref, b_out), (c_ref, c_out))
    copies = [pltpu.make_async_copy(x, y, sems.at[n]) for n, (x, y) in enumerate(pairs)]
    for copy in copies:
        copy.start()
    for copy in copies:
        copy.wait()


def local(tensor, building_factor, hour_weights):
    n_smp = lax.axis_size("smp")
    n_bld = lax.axis_size("bld")
    hours, n_i, n_j = tensor.shape
    rank = building_factor.shape[0]
    assert (n_smp, n_bld, rank, hours) == (8, 16, 64, 4)
    i_share, j_share = n_i // n_bld, n_j // n_smp
    assert (i_share, j_share) == (64, 128)
    f32, bf16 = jnp.float32, jnp.bfloat16
    body = functools.partial(kernel, n_smp, n_bld, n_i * n_smp, n_j * n_bld)
    vmem = pl.BlockSpec(memory_space=pltpu.VMEM)
    pad = 8
    results = pl.pallas_call(
        body,
        out_shape=(
            jax.ShapeDtypeStruct((rank, i_share), f32),
            jax.ShapeDtypeStruct((rank, j_share), f32),
            jax.ShapeDtypeStruct((hours, rank), f32),
        ),
        in_specs=[pl.BlockSpec(memory_space=pl.ANY), vmem, vmem],
        out_specs=(vmem, vmem, vmem),
        scratch_shapes=[
            pltpu.VMEM((hours, n_i, n_j), bf16),
            pltpu.VMEM((hours, rank, n_j), f32),
            pltpu.VMEM((hours, rank, n_i), f32),
            pltpu.VMEM((hours, n_bld // 2, rank // 2, 2 * i_share), f32),
            pltpu.VMEM((hours, n_bld // 2, rank // 2, 2 * i_share), bf16),
            pltpu.VMEM((hours, n_bld // 2, rank // 2, 2 * i_share), bf16),
            pltpu.VMEM((rank // 2, 2 * rank), f32),
            pltpu.VMEM((rank // 2, 2 * rank), f32),
            pltpu.VMEM((rank // 2, 2 * i_share), f32),
            pltpu.VMEM((rank, j_share), f32),
            pltpu.VMEM((rank, 2 * rank), f32),
            pltpu.VMEM((rank, 2 * rank), f32),
            pltpu.VMEM((rank, 2 * rank), f32),
            pltpu.VMEM((rank, 2 * rank), f32),
            pltpu.VMEM((pad, 2 * rank), f32),
            pltpu.VMEM((rank, pad), f32),
            pltpu.VMEM((rank, pad), f32),
            pltpu.VMEM((pad, 2 * rank), f32),
            pltpu.VMEM((rank, pad), f32),
            pltpu.VMEM((hours, n_bld // 2, rank // 2, 2 * i_share), bf16),
            pltpu.VMEM((hours, n_bld // 2, rank // 2, 2 * i_share), bf16),
            pltpu.VMEM((rank // 2, 2 * i_share), bf16),
            pltpu.VMEM((n_bld, rank // 2, 2 * i_share), bf16),
            pltpu.VMEM((rank // 2, 2 * rank), f32),
            pltpu.VMEM((n_smp, rank // 2, 2 * rank), f32),
            pltpu.VMEM((n_smp, rank, j_share), bf16),
            pltpu.VMEM((n_smp, rank, j_share), bf16),
            pltpu.VMEM((rank, j_share), bf16),
            pltpu.VMEM((n_smp, rank, j_share), bf16),
            pltpu.VMEM((rank // 2, 2 * rank), f32),
            pltpu.VMEM((n_bld // 2, rank // 2, 2 * rank), f32),
            pltpu.VMEM((rank // 2, 2 * rank), f32),
            pltpu.VMEM((n_bld, rank // 2, 2 * rank), f32),
            pltpu.VMEM((pad, 2 * rank), f32),
            pltpu.VMEM((n_bld, pad, 2 * rank), f32),
            pltpu.VMEM((pad, 2 * rank), f32),
            pltpu.VMEM((n_smp, pad, 2 * rank), f32),
            pltpu.SemaphoreType.DMA((hours,)),
            pltpu.SemaphoreType.DMA((COUNT,)),
            pltpu.SemaphoreType.DMA((COUNT,)),
        ],
        compiler_params=pltpu.CompilerParams(
            collective_id=0, has_side_effects=True, vmem_limit_bytes=60 * 1024 * 1024
        ),
        name="als_sweeps",
    )(tensor, building_factor, hour_weights)
    return pl.pallas_call(
        put_out,
        out_shape=tuple(jax.ShapeDtypeStruct(x.shape, x.dtype) for x in results),
        in_specs=[vmem] * 3,
        out_specs=(pl.BlockSpec(memory_space=pl.ANY),) * 3,
        scratch_shapes=[pltpu.SemaphoreType.DMA((3,))],
        name="put_out",
    )(*results)


def solution(mesh):
    in_specs = (P(None, "smp", "bld"), P(None, "bld"), P())
    out_specs = (P(None, ("smp", "bld")), P(None, ("bld", "smp")), P())
    return jax.shard_map(local, mesh=mesh, in_specs=in_specs, out_specs=out_specs, check_vma=False)
```

```python
import functools
import math

import jax
import jax.numpy as jnp
from jax import lax
from jax.experimental import pallas as pl
from jax.experimental.pallas import tpu as pltpu
from jax.sharding import PartitionSpec as P

SWEEPS = 5
EPSILON = 1e-06
RIDGE_SHARE = 0.05
HIGHEST = lax.Precision.HIGHEST
MESH = pl.DeviceIdType.MESH
NT = (((1,), (1,)), ((), ()))
NN = (((1,), (0,)), ((), ()))

BLD_STEPS = [
    (dy, dx, dc) for dy in (2, 1, 3, 0) for dx in (1, 0) for dc in (1, 0) if (dy, dx, dc) != (0, 0, 0)
]
SMP_STEPS = [(dx, dz) for dz in (2, 1, 3, 0) for dx in (1, 0) if (dx, dz) != (0, 0)]


def dot32(a, b, dims=NN):
    return lax.dot_general(a, b, dims, precision=HIGHEST, preferred_element_type=jnp.float32)


def dot16(a, b, dims=NN):
    return lax.dot_general(a, b, dims, preferred_element_type=jnp.float32)


def identity(n):
    rows = lax.broadcasted_iota(jnp.int32, (n, n), 0)
    cols = lax.broadcasted_iota(jnp.int32, (n, n), 1)
    return (rows == cols).astype(jnp.float32)


def pack(square):
    half = square.shape[0] // 2
    return jnp.concatenate([square[:half], square[half:]], axis=1)


def low_lanes(rows):
    return lax.broadcasted_iota(jnp.int32, (rows, 128), 1) < 64


def unpack_twice(packed):
    turned = pltpu.roll(packed, 64, 1)
    low = low_lanes(packed.shape[0])
    return jnp.concatenate([jnp.where(low, packed, turned), jnp.where(low, turned, packed)], axis=0)


def identity_twice(n):
    rows = lax.broadcasted_iota(jnp.int32, (n, 2 * n), 0)
    cols = lax.broadcasted_iota(jnp.int32, (n, 2 * n), 1)
    return ((cols == rows) | (cols == rows + n)).astype(jnp.float32)


def split(x):
    high = x.astype(jnp.bfloat16).astype(jnp.float32)
    rest = x - high
    middle = rest.astype(jnp.bfloat16).astype(jnp.float32)
    return high, middle, rest - middle


def low16(*arrays):
    return [array.astype(jnp.bfloat16) for array in arrays]


def left_parts(a):
    high, middle, rest = split(a)
    low = low_lanes(a.shape[0])
    one = jnp.concatenate(low16(high, jnp.where(low, middle, high)), axis=1)
    two = jnp.where(low, rest, middle).astype(jnp.bfloat16)
    return one, two


def product(a, b):
    one, two = left_parts(a)
    high, middle, rest = low16(*split(b))
    return dot16(one, jnp.concatenate([high, middle, high, rest], axis=0)) + dot16(
        two, jnp.concatenate([high, middle], axis=0)
    )


def regularized_inverse(gram):
    n = gram.shape[0]
    eye = identity_twice(n)
    mean = jnp.sum(jnp.sum(gram * eye, axis=0, keepdims=True), axis=1, keepdims=True) / (2 * n)
    scale = 2.0 / ((n + 2 * RIDGE_SHARE) * mean)
    t = scale * (gram + RIDGE_SHARE * mean * eye)
    y = None
    spread = n / (n + 2 * RIDGE_SHARE)
    steps = 8
    for step in range(steps):
        spread = spread * spread / (2.0 - spread * spread)
        gain = 1.0 + spread
        factor = gain * (2.0 * eye - t)
        if step == 0:
            y = factor
            t = product(t, factor)
        elif step < steps - 1:
            both = product(jnp.concatenate([y, t], axis=0), factor)
            y, t = both[:n], both[n:]
        else:
            y = product(y, factor)
    return scale * y


def scales_of(gram_raw, count):
    n = gram_raw.shape[0]
    diagonal = gram_raw * identity_twice(n)
    inv_row = 1.0 / jnp.sqrt(jnp.sum(diagonal, axis=0, keepdims=True) / count + EPSILON)
    inv_col = 1.0 / jnp.sqrt(jnp.sum(diagonal, axis=1, keepdims=True) / (2 * count) + EPSILON)
    return inv_row, inv_col


RS1, AG1, AG2, PAIR, GS, RS2, GB, P1, P2, GB0, GP, COUNT = 0, 4, 8, 12, 16, 17, 18, 19, 20, 21, 22, 23


def kernel(
    n_smp, n_bld, samples_total, buildings_total,
    tensor_ref, build_ref, hour_ref,
    sample_out, build_out, hour_out,
    slab, mixed, partial, factor, own, pair_send, pair_recv, gp_send, gp_recv, s_slice, b_slice,
    gram_build, gram_sample, inv_sample, inv_build, inv_hour, hour_rhs, hour_cols, inv_b_col, inv_s_row, inv_s_col,
    rs1_send, rs1_recv, ag1_send, ag1_recv, gs_send, gs_recv,
    rs2_send, rs2_recv, ag2_send, ag2_recv, gb_send, gb_recv, gb0_send, gb0_recv, p1_send, p1_recv, p2_send, p2_recv,
    load_sem, send_sems, recv_sems,
):
    hours, n_i, n_j = slab.shape
    rank = build_ref.shape[0]
    half = rank // 2
    scale_up = math.sqrt(samples_total * buildings_total)
    smp = lax.axis_index("smp")
    bld = lax.axis_index("bld")
    core = bld % 2
    x_hi = (bld // 2) % 2
    y = bld // 4
    z = smp % 4
    x_lo = smp // 4

    def bld_peer(step):
        dy, dx, dc = step
        return ((y + dy) % 4) * 4 + ((x_hi + dx) % 2) * 2 + (core + dc) % 2

    def smp_peer(step):
        dx, dz = step
        return ((x_lo + dx) % 2) * 4 + (z + dz) % 4

    bld_peers = [bld_peer(step) for step in BLD_STEPS]
    like_steps = [step for step in BLD_STEPS if step[2] == 0]
    like_peers = [bld_peer(step) for step in like_steps]
    partner = bld_peer((0, 0, 1))
    chip = bld // 2
    n_chip = n_bld // 2
    smp_peers = [smp_peer(step) for step in SMP_STEPS]

    def start_exchange(axis, piece_of, place, sem_of):
        if axis == "like":
            peers, steps, axis = like_peers, like_steps, "bld"
        elif axis == "partner":
            peers, steps, axis = [partner], [(0, 0, 1)], "bld"
        elif axis == "bld":
            peers, steps = bld_peers, BLD_STEPS
        else:
            peers, steps = smp_peers, SMP_STEPS
        for peer, step in zip(peers, steps):
            pltpu.make_async_remote_copy(
                src_ref=piece_of(peer),
                dst_ref=place,
                send_sem=send_sems.at[sem_of(step)],
                recv_sem=recv_sems.at[sem_of(step)],
                device_id={axis: peer},
                device_id_type=MESH,
            ).start()

    def finish_exchange(sem, pieces):
        done = pltpu.make_async_remote_copy(
            src_ref=pieces,
            dst_ref=pieces,
            send_sem=send_sems.at[sem],
            recv_sem=recv_sems.at[sem],
            device_id={"bld": bld_peers[0]},
            device_id_type=MESH,
        )
        done.wait_recv()
        done.wait_send()

    barrier = pltpu.get_barrier_semaphore()
    for peer in bld_peers:
        pl.semaphore_signal(barrier, inc=1, device_id={"bld": peer}, device_id_type=MESH)
    for peer in smp_peers:
        pl.semaphore_signal(barrier, inc=1, device_id={"smp": peer}, device_id_type=MESH)

    def place(s):
        return (s % 4) * 2 + s // 4

    def load(k, s):
        from_ref = tensor_ref.at[k, :, s * 128 : (s + 1) * 128]
        to_ref = slab.at[k, :, place(s) * 128 : (place(s) + 1) * 128]
        return pltpu.make_async_copy(from_ref, to_ref, load_sem.at[k, s])

    for k in range(hours):
        for s in range(n_smp):
            load(k, s).start()

    low_lane = low_lanes(half)
    tile = 512

    def scatter(k, i, block):
        for m in range(tile // 128):
            top, low = block[:half, m * 128 : (m + 1) * 128], block[half:, m * 128 : (m + 1) * 128]
            moved = pltpu.roll(jnp.where(low_lane, low, top), 64, 1)
            even = jnp.where(low_lane, top, moved)
            odd = jnp.where(low_lane, moved, low)
            own[k, i // 128 + m] = jnp.where(core == 0, even, odd)
            pair_send[k, i // 128 + m] = jnp.where(core == 0, odd, even).astype(pair_send.dtype)

    def pair_start(k):
        start_exchange("partner", lambda peer: pair_send.at[k], pair_recv.at[k], lambda step: PAIR + k)

    def pair_finish(k):
        finish_exchange(PAIR + k, pair_recv.at[k])
        for c in range(n_chip):
            rs1_send[k, c] = (own[k, c] + pair_recv[k, c].astype(jnp.float32)).astype(rs1_send.dtype)
        rs1_recv[k, chip] = rs1_send[k, chip]
        start_exchange("like", lambda peer: rs1_send.at[k, peer // 2], rs1_recv.at[k, chip], lambda step: RS1 + k)

    def slices(ref, index, groups):
        parts = [ref[index + (pl.ds(pl.multiple_of(group * 256, 256), 256),)] for group in groups]
        return parts[0] if len(parts) == 1 else jnp.concatenate(parts, axis=-1)

    def gathered(group):
        return jnp.concatenate([ag2_recv[group], ag2_recv[4 + group]], axis=1)

    def solve_columns(parts, columns):
        solved = dot16(parts, columns)
        solved = solved[:rank] + (solved[rank : 2 * rank] + solved[2 * rank :])
        return solved.astype(jnp.bfloat16)

    def project(k, i, groups):
        return dot16(slices(factor, (slice(None),), groups), slices(slab, (k, slice(i, i + tile)), groups), NT)

    def build_gram_start(gram, send, recv, sem):
        message = pack(gram)
        send[...] = message
        recv[bld] = message
        start_exchange("bld", lambda peer: send, recv.at[bld], lambda step: sem)

    def build_gram_finish(recv, sem):
        others = recv.shape[0] - 1
        finish_exchange(sem, recv.at[pl.ds(0, others)])
        total = recv[0]
        for b in range(1, others + 1):
            total = total + recv[b]
        return unpack_twice(total)

    pad = hour_rhs.shape[0]
    pick_rows = lax.broadcasted_iota(jnp.int32, (pad, 128), 0)
    quarter = lax.broadcasted_iota(jnp.int32, (pad, 128), 1) // 32
    held = jnp.where(quarter == 0, 2, jnp.where(quarter == 1, 0, jnp.where(quarter == 2, 3, 1)))
    pick = (pick_rows == held).astype(jnp.bfloat16)

    def lane_sums(sums):
        low = low_lanes(rank)
        folded = [x + pltpu.roll(x, 64, 1) for x in sums]
        first = jnp.where(low, folded[0], folded[1])
        second = jnp.where(low, folded[2], folded[3])
        first = first + pltpu.roll(first, 32, 1)
        second = second + pltpu.roll(second, 96, 1)
        upper = (lax.broadcasted_iota(jnp.int32, (rank, 128), 1) // 32) % 2 == 1
        parts = low16(*split(jnp.where(upper, first, second)))
        rows = dot16(jnp.concatenate([pick] * 3, axis=1), jnp.concatenate(parts, axis=1), NT)
        return jnp.concatenate([rows, rows], axis=1)

    hour_rhs[...] = jnp.zeros_like(hour_rhs)
    hour_rhs[0:hours, 0:rank] = hour_ref[...] / scale_up
    inv_hour[...] = identity_twice(rank)
    hour_cols[...] = dot32(identity(rank), hour_rhs[:, 0:rank], NT)
    inv_b_col[...] = jnp.ones_like(inv_b_col)
    order_of = sorted(range(n_smp), key=place)
    start_factor = jnp.concatenate(
        [build_ref[:, s * 128 : (s + 1) * 128] for s in order_of], axis=1
    ).astype(jnp.bfloat16)
    for k in range(hours):
        for s in range(n_smp):
            load(k, s).wait()
        for i in range(0, n_i, tile):
            scatter(k, i, dot16(start_factor, slab[k, i : i + tile, :], NT))
        if k == 1:
            pl.semaphore_wait(barrier, n_bld + n_smp - 2)
            pair_start(0)
        if k >= 1:
            pair_start(k)
            pair_finish(k - 1)
    pair_finish(hours - 1)
    build_gram_start(dot32(build_ref[...], build_ref[...], NT), gb0_send, gb0_recv, GB0)

    @pl.loop(0, SWEEPS)
    def _(sweep):
        for k in range(hours):
            finish_exchange(RS1 + k, rs1_recv.at[k, pl.ds(0, n_chip - 1)])
        right = None
        for k in range(hours):
            col = hour_cols[:, k : k + 1] * inv_b_col[:, 0:1]
            both = jnp.where(
                low_lane,
                jnp.broadcast_to(col[:half], (half, 128)),
                jnp.broadcast_to(col[half:], (half, 128)),
            )
            total = rs1_recv[k, 0].astype(jnp.float32)
            for c in range(1, n_chip):
                total = total + rs1_recv[k, c].astype(jnp.float32)
            right = both * total if right is None else right + both * total
        s_slice[...] = right
        message = right.astype(jnp.bfloat16)
        ag1_send[...] = message
        ag1_recv[bld] = message
        start_exchange("bld", lambda peer: ag1_send, ag1_recv.at[bld], lambda step: AG1 + step[0])

        @pl.when(sweep == 0)
        def _():
            gram_build[...] = build_gram_finish(gb0_recv, GB0)

        gram_hour = dot32(hour_cols[...], dot32(hour_rhs[:, 0:rank], inv_hour[...]))
        inverse = regularized_inverse(gram_build[...] * gram_hour)
        inv_sample[...] = inverse
        parts = jnp.concatenate(low16(*split(inverse)), axis=0)[:, :rank]
        gram_part = jnp.zeros((rank, rank), jnp.float32)

        for order, steps in enumerate(((0,), (1, 3), (2,))):
            chunks = [(y - dy + 4) % 4 for dy in steps]
            columns = []
            for dy, chunk in zip(steps, chunks):
                finish_exchange(AG1 + dy, ag1_recv.at[pl.ds(0, 3 if dy == 0 else 4)])
                for m in range(2):
                    even = ag1_recv[chunk * 4 + 2 * m].astype(jnp.float32)
                    odd = ag1_recv[chunk * 4 + 2 * m + 1].astype(jnp.float32)
                    moved = pltpu.roll(jnp.where(low_lane, odd, even), 64, 1)
                    top = jnp.where(low_lane, even, moved)
                    low = jnp.where(low_lane, moved, odd)
                    columns.append(jnp.concatenate([top, low], axis=0).astype(jnp.bfloat16))
            solved = solve_columns(parts, jnp.concatenate(columns, axis=1))
            rows = [pl.ds(pl.multiple_of(chunk * 256, 256), 256) for chunk in chunks]
            if order < 2:
                gram_part = gram_part + dot16(solved, solved, NT)
            for k in range(hours):
                for j in range(0, n_j, tile):
                    block = jnp.concatenate([slab[k, rows_of, j : j + tile] for rows_of in rows], axis=0)
                    block = dot16(solved, block)
                    if order == 0:
                        mixed[k, :, j : j + tile] = block
                    else:
                        mixed[k, :, j : j + tile] += block

        cols = [jnp.broadcast_to(hour_cols[:, k : k + 1], (rank, 128)) for k in range(hours)]
        for s in range(n_smp):
            at = place(s) * 128
            block = cols[0] * mixed[0, :, at : at + 128]
            for k in range(1, hours):
                block = block + cols[k] * mixed[k, :, at : at + 128]
            rs2_send[s] = block.astype(rs2_send.dtype)
        rs2_recv[smp] = rs2_send[smp]
        start_exchange("smp", lambda peer: rs2_send.at[peer], rs2_recv.at[smp], lambda step: RS2)

        message = pack(gram_part + dot16(solved, solved, NT))
        gs_send[...] = message
        gs_recv[smp] = message
        start_exchange("smp", lambda peer: gs_send, gs_recv.at[smp], lambda step: GS)

        finish_exchange(RS2, rs2_recv.at[pl.ds(0, n_smp - 1)])
        total = rs2_recv[0].astype(jnp.float32)
        for s in range(1, n_smp):
            total = total + rs2_recv[s].astype(jnp.float32)
        b_slice[...] = total
        message = total.astype(jnp.bfloat16)
        ag2_send[...] = message
        ag2_recv[smp] = message
        start_exchange("smp", lambda peer: ag2_send, ag2_recv.at[smp], lambda step: AG2 + step[1])

        finish_exchange(GS, gs_recv.at[pl.ds(0, n_smp - 1)])
        gram_raw = gs_recv[0]
        for s in range(1, n_smp):
            gram_raw = gram_raw + gs_recv[s]
        gram_raw = unpack_twice(gram_raw)
        inv_row, inv_col = scales_of(gram_raw, samples_total)
        inv_s_row[...] = jnp.broadcast_to(inv_row, inv_s_row.shape)
        inv_s_col[...] = jnp.broadcast_to(inv_col, inv_s_col.shape)
        gram_sample[...] = gram_raw * (inv_col * inv_row)
        inverse = regularized_inverse(gram_sample[...] * gram_hour) * inv_row
        inv_build[...] = inverse
        parts = jnp.concatenate(low16(*split(inverse)), axis=0)[:, :rank]

        sums = [jnp.zeros((rank, 128), jnp.float32) for _ in range(hours)]
        gram_part = jnp.zeros((rank, rank), jnp.float32)
        before_last = sweep < SWEEPS - 1
        groups = [(z - dz + 4) % 4 for dz in (0, 1, 3, 2)]
        early = {k: groups[:2] if k < 2 else groups[:1] for k in range(hours)}
        for order, dz in enumerate((0, 1, 3, 2)):
            finish_exchange(AG2 + dz, ag2_recv.at[pl.ds(0, 1 if dz == 0 else 2)])
            group = groups[order]
            solved = solve_columns(parts, gathered(group))
            factor[:, pl.ds(pl.multiple_of(group * 256, 256), 256)] = solved
            gram_part = gram_part + dot16(solved, solved, NT)
            wide = solved.astype(jnp.float32)
            for k in range(hours):
                terms = slices(mixed, (k, slice(None)), [group]) * wide
                sums[k] = sums[k] + (terms[:, :128] + terms[:, 128:])
            if order < 2:

                @pl.when(before_last)
                def _():
                    for k in range(hours):
                        if order < len(early[k]):
                            for i in range(0, n_i, tile):
                                block = project(k, i, [group])
                                if order == 0:
                                    partial[k, :, i : i + tile] = block
                                else:
                                    partial[k, :, i : i + tile] += block

        message = lane_sums(sums)
        p1_send[...] = message
        p1_recv[bld] = message
        start_exchange("bld", lambda peer: p1_send, p1_recv.at[bld], lambda step: P1)
        message = pack(gram_part)
        gp_send[...] = message
        start_exchange("partner", lambda peer: gp_send, gp_recv, lambda step: GP)

        def finish_project(k):
            left = groups[len(early[k]) :]
            for i in range(0, n_i, tile):
                scatter(k, i, partial[k, :, i : i + tile] + project(k, i, left))
            pair_start(k)

        @pl.when(before_last)
        def _():
            finish_project(0)

        finish_exchange(GP, gp_recv)
        message = gp_send[...] + gp_recv[...]
        gb_send[...] = message
        gb_recv[chip] = message
        start_exchange("like", lambda peer: gb_send, gb_recv.at[chip], lambda step: GB)

        @pl.when(before_last)
        def _():
            for k in range(1, hours):
                finish_project(k)
                pair_finish(k - 1)
            pair_finish(hours - 1)

        rows = p1_recv.shape[0]
        finish_exchange(P1, p1_recv.at[pl.ds(0, rows - 1)])
        total = p1_recv[0]
        for n in range(1, rows):
            total = total + p1_recv[n]
        p2_send[...] = total
        p2_recv[smp] = total
        start_exchange("smp", lambda peer: p2_send, p2_recv.at[smp], lambda step: P2)

        gram_raw = build_gram_finish(gb_recv, GB)
        inv_row, inv_col = scales_of(gram_raw, buildings_total)
        inv_b_col[...] = jnp.broadcast_to(inv_col, inv_b_col.shape)
        gram_build[...] = gram_raw * (inv_col * inv_row)
        inverse = regularized_inverse(gram_sample[...] * gram_build[...])
        inv_hour[...] = inverse
        one, two = left_parts(inverse)
        scale_row = inv_row * inv_s_row[0:1, :]

        planes = p2_recv.shape[0]
        finish_exchange(P2, p2_recv.at[pl.ds(0, planes - 1)])
        total = p2_recv[0]
        for n in range(1, planes):
            total = total + p2_recv[n]
        right = total * scale_row
        hour_rhs[...] = right
        high, middle, rest = split(right)
        low = low_lanes(pad)
        both = jnp.where(low, high, middle).astype(jnp.bfloat16)
        far = jnp.where(low, high, rest).astype(jnp.bfloat16)
        hour_cols[...] = dot16(one, jnp.concatenate([both, far], axis=1), NT) + dot16(two, both, NT)

    sample_out[...] = product(inv_sample[...], unpack_twice(s_slice[...]))[:, :rank] * inv_s_col[:, 0:1]
    build_out[...] = product(inv_build[...], b_slice[...]) * inv_b_col[:, 0:1]
    hour_out[...] = dot32(hour_rhs[:, 0:rank], inv_hour[:, 0:rank])[0:hours] * scale_up


def put_out(a_ref, b_ref, c_ref, a_out, b_out, c_out, sems):
    pairs = ((a_ref, a_out), (b_ref, b_out), (c_ref, c_out))
    copies = [pltpu.make_async_copy(x, y, sems.at[n]) for n, (x, y) in enumerate(pairs)]
    for copy in copies:
        copy.start()
    for copy in copies:
        copy.wait()


def local(tensor, building_factor, hour_weights):
    n_smp = lax.axis_size("smp")
    n_bld = lax.axis_size("bld")
    hours, n_i, n_j = tensor.shape
    rank = building_factor.shape[0]
    assert (n_smp, n_bld, rank, hours) == (8, 16, 64, 4)
    i_share, j_share = n_i // n_bld, n_j // n_smp
    assert (i_share, j_share) == (64, 128)
    f32, bf16 = jnp.float32, jnp.bfloat16
    body = functools.partial(kernel, n_smp, n_bld, n_i * n_smp, n_j * n_bld)
    vmem = pl.BlockSpec(memory_space=pltpu.VMEM)
    pad = 8
    results = pl.pallas_call(
        body,
        out_shape=(
            jax.ShapeDtypeStruct((rank, i_share), f32),
            jax.ShapeDtypeStruct((rank, j_share), f32),
            jax.ShapeDtypeStruct((hours, rank), f32),
        ),
        in_specs=[pl.BlockSpec(memory_space=pl.ANY), vmem, vmem],
        out_specs=(vmem, vmem, vmem),
        scratch_shapes=[
            pltpu.VMEM((hours, n_i, n_j), bf16),
            pltpu.VMEM((hours, rank, n_j), f32),
            pltpu.VMEM((hours, rank, n_i), f32),
            pltpu.VMEM((rank, n_j), bf16),
            pltpu.VMEM((hours, n_bld // 2, rank // 2, 2 * i_share), f32),
            pltpu.VMEM((hours, n_bld // 2, rank // 2, 2 * i_share), bf16),
            pltpu.VMEM((hours, n_bld // 2, rank // 2, 2 * i_share), bf16),
            pltpu.VMEM((rank // 2, 2 * rank), f32),
            pltpu.VMEM((rank // 2, 2 * rank), f32),
            pltpu.VMEM((rank // 2, 2 * i_share), f32),
            pltpu.VMEM((rank, j_share), f32),
            pltpu.VMEM((rank, 2 * rank), f32),
            pltpu.VMEM((rank, 2 * rank), f32),
            pltpu.VMEM((rank, 2 * rank), f32),
            pltpu.VMEM((rank, 2 * rank), f32),
            pltpu.VMEM((rank, 2 * rank), f32),
            pltpu.VMEM((pad, 2 * rank), f32),
            pltpu.VMEM((rank, pad), f32),
            pltpu.VMEM((rank, pad), f32),
            pltpu.VMEM((pad, 2 * rank), f32),
            pltpu.VMEM((rank, pad), f32),
            pltpu.VMEM((hours, n_bld // 2, rank // 2, 2 * i_share), bf16),
            pltpu.VMEM((hours, n_bld // 2, rank // 2, 2 * i_share), bf16),
            pltpu.VMEM((rank // 2, 2 * i_share), bf16),
            pltpu.VMEM((n_bld, rank // 2, 2 * i_share), bf16),
            pltpu.VMEM((rank // 2, 2 * rank), f32),
            pltpu.VMEM((n_smp, rank // 2, 2 * rank), f32),
            pltpu.VMEM((n_smp, rank, j_share), bf16),
            pltpu.VMEM((n_smp, rank, j_share), bf16),
            pltpu.VMEM((rank, j_share), bf16),
            pltpu.VMEM((n_smp, rank, j_share), bf16),
            pltpu.VMEM((rank // 2, 2 * rank), f32),
            pltpu.VMEM((n_bld // 2, rank // 2, 2 * rank), f32),
            pltpu.VMEM((rank // 2, 2 * rank), f32),
            pltpu.VMEM((n_bld, rank // 2, 2 * rank), f32),
            pltpu.VMEM((pad, 2 * rank), f32),
            pltpu.VMEM((n_bld, pad, 2 * rank), f32),
            pltpu.VMEM((pad, 2 * rank), f32),
            pltpu.VMEM((n_smp, pad, 2 * rank), f32),
            pltpu.SemaphoreType.DMA((hours, n_smp)),
            pltpu.SemaphoreType.DMA((COUNT,)),
            pltpu.SemaphoreType.DMA((COUNT,)),
        ],
        compiler_params=pltpu.CompilerParams(
            collective_id=0, has_side_effects=True, vmem_limit_bytes=60 * 1024 * 1024
        ),
        name="als_sweeps",
    )(tensor, building_factor, hour_weights)
    return pl.pallas_call(
        put_out,
        out_shape=tuple(jax.ShapeDtypeStruct(x.shape, x.dtype) for x in results),
        in_specs=[vmem] * 3,
        out_specs=(pl.BlockSpec(memory_space=pl.ANY),) * 3,
        scratch_shapes=[pltpu.SemaphoreType.DMA((3,))],
        name="put_out",
    )(*results)


def solution(mesh):
    in_specs = (P(None, "smp", "bld"), P(None, "bld"), P())
    out_specs = (P(None, ("smp", "bld")), P(None, ("bld", "smp")), P())
    return jax.shard_map(local, mesh=mesh, in_specs=in_specs, out_specs=out_specs, check_vma=False)
```

```python
import functools
import math

import jax
import jax.numpy as jnp
from jax import lax
from jax.experimental import pallas as pl
from jax.experimental.pallas import tpu as pltpu
from jax.sharding import PartitionSpec as P

SWEEPS = 5
EPSILON = 1e-06
RIDGE_SHARE = 0.05
HIGHEST = lax.Precision.HIGHEST
MESH = pl.DeviceIdType.MESH
NT = (((1,), (1,)), ((), ()))
NN = (((1,), (0,)), ((), ()))

BLD_STEPS = [
    (dy, dx, dc) for dy in (2, 1, 3, 0) for dx in (1, 0) for dc in (1, 0) if (dy, dx, dc) != (0, 0, 0)
]
SMP_STEPS = [(dx, dz) for dz in (2, 1, 3, 0) for dx in (1, 0) if (dx, dz) != (0, 0)]


def dot32(a, b, dims=NN):
    return lax.dot_general(a, b, dims, precision=HIGHEST, preferred_element_type=jnp.float32)


def dot16(a, b, dims=NN):
    return lax.dot_general(a, b, dims, preferred_element_type=jnp.float32)


def identity(n):
    rows = lax.broadcasted_iota(jnp.int32, (n, n), 0)
    cols = lax.broadcasted_iota(jnp.int32, (n, n), 1)
    return (rows == cols).astype(jnp.float32)


def pack(square):
    half = square.shape[0] // 2
    return jnp.concatenate([square[:half], square[half:]], axis=1)


def low_lanes(rows):
    return lax.broadcasted_iota(jnp.int32, (rows, 128), 1) < 64


def unpack_twice(packed):
    turned = pltpu.roll(packed, 64, 1)
    low = low_lanes(packed.shape[0])
    return jnp.concatenate([jnp.where(low, packed, turned), jnp.where(low, turned, packed)], axis=0)


def identity_twice(n):
    rows = lax.broadcasted_iota(jnp.int32, (n, 2 * n), 0)
    cols = lax.broadcasted_iota(jnp.int32, (n, 2 * n), 1)
    return ((cols == rows) | (cols == rows + n)).astype(jnp.float32)


def split(x):
    high = x.astype(jnp.bfloat16).astype(jnp.float32)
    rest = x - high
    middle = rest.astype(jnp.bfloat16).astype(jnp.float32)
    return high, middle, rest - middle


def low16(*arrays):
    return [array.astype(jnp.bfloat16) for array in arrays]


def left_parts(a):
    high, middle, rest = split(a)
    low = low_lanes(a.shape[0])
    one = jnp.concatenate(low16(high, jnp.where(low, middle, high)), axis=1)
    two = jnp.where(low, rest, middle).astype(jnp.bfloat16)
    return one, two


def product(a, b):
    one, two = left_parts(a)
    high, middle, rest = low16(*split(b))
    return dot16(one, jnp.concatenate([high, middle, high, rest], axis=0)) + dot16(
        two, jnp.concatenate([high, middle], axis=0)
    )


def regularized_inverse(gram):
    n = gram.shape[0]
    eye = identity_twice(n)
    mean = jnp.sum(jnp.sum(gram * eye, axis=0, keepdims=True), axis=1, keepdims=True) / (2 * n)
    scale = 2.0 / ((n + 2 * RIDGE_SHARE) * mean)
    t = scale * (gram + RIDGE_SHARE * mean * eye)
    y = None
    spread = n / (n + 2 * RIDGE_SHARE)
    steps = 8
    for step in range(steps):
        spread = spread * spread / (2.0 - spread * spread)
        gain = 1.0 + spread
        factor = gain * (2.0 * eye - t)
        if step == 0:
            y = factor
            t = product(t, factor)
        elif step < steps - 1:
            both = product(jnp.concatenate([y, t], axis=0), factor)
            y, t = both[:n], both[n:]
        else:
            y = product(y, factor)
    return scale * y


def scales_of(gram_raw, count):
    n = gram_raw.shape[0]
    diagonal = gram_raw * identity_twice(n)
    inv_row = 1.0 / jnp.sqrt(jnp.sum(diagonal, axis=0, keepdims=True) / count + EPSILON)
    inv_col = 1.0 / jnp.sqrt(jnp.sum(diagonal, axis=1, keepdims=True) / (2 * count) + EPSILON)
    return inv_row, inv_col


RS1, AG1, AG2, PAIR, GS, RS2, GB, P1, P2, GB0, GP, COUNT = 0, 4, 8, 12, 16, 17, 18, 19, 20, 21, 22, 23


def kernel(
    n_smp, n_bld, samples_total, buildings_total,
    tensor_ref, build_ref, hour_ref,
    sample_out, build_out, hour_out,
    slab, mixed, partial, factor, own, pair_send, pair_recv, gp_send, gp_recv, s_slice, b_slice,
    gram_build, gram_sample, inv_sample, inv_build, inv_hour, hour_rhs, hour_cols, inv_b_col, inv_s_row, inv_s_col,
    rs1_send, rs1_recv, ag1_send, ag1_recv, gs_send, gs_recv,
    rs2_send, rs2_recv, ag2_send, ag2_recv, gb_send, gb_recv, gb0_send, gb0_recv, p1_send, p1_recv, p2_send, p2_recv,
    load_sem, send_sems, recv_sems,
):
    hours, n_i, n_j = slab.shape
    rank = build_ref.shape[0]
    half = rank // 2
    scale_up = math.sqrt(samples_total * buildings_total)
    smp = lax.axis_index("smp")
    bld = lax.axis_index("bld")
    core = bld % 2
    x_hi = (bld // 2) % 2
    y = bld // 4
    z = smp % 4
    x_lo = smp // 4

    def bld_peer(step):
        dy, dx, dc = step
        return ((y + dy) % 4) * 4 + ((x_hi + dx) % 2) * 2 + (core + dc) % 2

    def smp_peer(step):
        dx, dz = step
        return ((x_lo + dx) % 2) * 4 + (z + dz) % 4

    bld_peers = [bld_peer(step) for step in BLD_STEPS]
    like_steps = [step for step in BLD_STEPS if step[2] == 0]
    like_peers = [bld_peer(step) for step in like_steps]
    partner = bld_peer((0, 0, 1))
    chip = bld // 2
    n_chip = n_bld // 2
    smp_peers = [smp_peer(step) for step in SMP_STEPS]

    def start_exchange(axis, piece_of, place, sem_of):
        if axis == "like":
            peers, steps, axis = like_peers, like_steps, "bld"
        elif axis == "partner":
            peers, steps, axis = [partner], [(0, 0, 1)], "bld"
        elif axis == "bld":
            peers, steps = bld_peers, BLD_STEPS
        else:
            peers, steps = smp_peers, SMP_STEPS
        for peer, step in zip(peers, steps):
            pltpu.make_async_remote_copy(
                src_ref=piece_of(peer),
                dst_ref=place,
                send_sem=send_sems.at[sem_of(step)],
                recv_sem=recv_sems.at[sem_of(step)],
                device_id={axis: peer},
                device_id_type=MESH,
            ).start()

    def finish_exchange(sem, pieces):
        done = pltpu.make_async_remote_copy(
            src_ref=pieces,
            dst_ref=pieces,
            send_sem=send_sems.at[sem],
            recv_sem=recv_sems.at[sem],
            device_id={"bld": bld_peers[0]},
            device_id_type=MESH,
        )
        done.wait_recv()
        done.wait_send()

    barrier = pltpu.get_barrier_semaphore()
    for peer in bld_peers:
        pl.semaphore_signal(barrier, inc=1, device_id={"bld": peer}, device_id_type=MESH)
    for peer in smp_peers:
        pl.semaphore_signal(barrier, inc=1, device_id={"smp": peer}, device_id_type=MESH)

    def place(s):
        return (s % 4) * 2 + s // 4

    def load(k, s):
        from_ref = tensor_ref.at[k, :, s * 128 : (s + 1) * 128]
        to_ref = slab.at[k, :, place(s) * 128 : (place(s) + 1) * 128]
        return pltpu.make_async_copy(from_ref, to_ref, load_sem.at[k, s])

    for k in range(hours):
        for s in range(n_smp):
            load(k, s).start()

    low_lane = low_lanes(half)
    tile = 512

    def scatter(k, i, block):
        for m in range(tile // 128):
            top, low = block[:half, m * 128 : (m + 1) * 128], block[half:, m * 128 : (m + 1) * 128]
            moved = pltpu.roll(jnp.where(low_lane, low, top), 64, 1)
            even = jnp.where(low_lane, top, moved)
            odd = jnp.where(low_lane, moved, low)
            own[k, i // 128 + m] = jnp.where(core == 0, even, odd)
            pair_send[k, i // 128 + m] = jnp.where(core == 0, odd, even).astype(pair_send.dtype)

    def pair_start(k):
        start_exchange("partner", lambda peer: pair_send.at[k], pair_recv.at[k], lambda step: PAIR + k)

    def pair_finish(k):
        finish_exchange(PAIR + k, pair_recv.at[k])
        for c in range(n_chip):
            rs1_send[k, c] = (own[k, c] + pair_recv[k, c].astype(jnp.float32)).astype(rs1_send.dtype)
        rs1_recv[k, chip] = rs1_send[k, chip]
        start_exchange("like", lambda peer: rs1_send.at[k, peer // 2], rs1_recv.at[k, chip], lambda step: RS1 + k)

    def slices(ref, index, groups):
        parts = [ref[index + (pl.ds(pl.multiple_of(group * 256, 256), 256),)] for group in groups]
        return parts[0] if len(parts) == 1 else jnp.concatenate(parts, axis=-1)

    def gathered(group):
        return jnp.concatenate([ag2_recv[group], ag2_recv[4 + group]], axis=1)

    def solve_columns(parts, columns):
        solved = dot16(parts, columns)
        solved = solved[:rank] + (solved[rank : 2 * rank] + solved[2 * rank :])
        return solved.astype(jnp.bfloat16)

    def project(k, i, groups):
        return dot16(slices(factor, (slice(None),), groups), slices(slab, (k, slice(i, i + tile)), groups), NT)

    def build_gram_start(gram, send, recv, sem):
        message = pack(gram)
        send[...] = message
        recv[bld] = message
        start_exchange("bld", lambda peer: send, recv.at[bld], lambda step: sem)

    def build_gram_finish(recv, sem):
        others = recv.shape[0] - 1
        finish_exchange(sem, recv.at[pl.ds(0, others)])
        total = recv[0]
        for b in range(1, others + 1):
            total = total + recv[b]
        return unpack_twice(total)

    pad = hour_rhs.shape[0]
    pick_rows = lax.broadcasted_iota(jnp.int32, (pad, 128), 0)
    quarter = lax.broadcasted_iota(jnp.int32, (pad, 128), 1) // 32
    held = jnp.where(quarter == 0, 2, jnp.where(quarter == 1, 0, jnp.where(quarter == 2, 3, 1)))
    pick = (pick_rows == held).astype(jnp.bfloat16)

    def lane_sums(sums):
        low = low_lanes(rank)
        folded = [x + pltpu.roll(x, 64, 1) for x in sums]
        first = jnp.where(low, folded[0], folded[1])
        second = jnp.where(low, folded[2], folded[3])
        first = first + pltpu.roll(first, 32, 1)
        second = second + pltpu.roll(second, 96, 1)
        upper = (lax.broadcasted_iota(jnp.int32, (rank, 128), 1) // 32) % 2 == 1
        parts = low16(*split(jnp.where(upper, first, second)))
        rows = dot16(jnp.concatenate([pick] * 3, axis=1), jnp.concatenate(parts, axis=1), NT)
        return jnp.concatenate([rows, rows], axis=1)

    hour_rhs[...] = jnp.zeros_like(hour_rhs)
    hour_rhs[0:hours, 0:rank] = hour_ref[...] / scale_up
    inv_hour[...] = identity_twice(rank)
    hour_cols[...] = dot32(identity(rank), hour_rhs[:, 0:rank], NT)
    inv_b_col[...] = jnp.ones_like(inv_b_col)
    order_of = sorted(range(n_smp), key=place)
    start_factor = jnp.concatenate(
        [build_ref[:, s * 128 : (s + 1) * 128] for s in order_of], axis=1
    ).astype(jnp.bfloat16)
    for k in range(hours):
        for s in range(n_smp):
            load(k, s).wait()
        for i in range(0, n_i, tile):
            scatter(k, i, dot16(start_factor, slab[k, i : i + tile, :], NT))
        if k == 1:
            pl.semaphore_wait(barrier, n_bld + n_smp - 2)
            pair_start(0)
        if k >= 1:
            pair_start(k)
            pair_finish(k - 1)
    pair_finish(hours - 1)
    build_gram_start(dot32(build_ref[...], build_ref[...], NT), gb0_send, gb0_recv, GB0)

    @pl.loop(0, SWEEPS)
    def _(sweep):
        for k in range(hours):
            finish_exchange(RS1 + k, rs1_recv.at[k, pl.ds(0, n_chip - 1)])
        right = None
        for k in range(hours):
            col = hour_cols[:, k : k + 1] * inv_b_col[:, 0:1]
            both = jnp.where(
                low_lane,
                jnp.broadcast_to(col[:half], (half, 128)),
                jnp.broadcast_to(col[half:], (half, 128)),
            )
            total = rs1_recv[k, 0].astype(jnp.float32)
            for c in range(1, n_chip):
                total = total + rs1_recv[k, c].astype(jnp.float32)
            right = both * total if right is None else right + both * total
        s_slice[...] = right
        message = right.astype(jnp.bfloat16)
        ag1_send[...] = message
        ag1_recv[bld] = message
        start_exchange("bld", lambda peer: ag1_send, ag1_recv.at[bld], lambda step: AG1 + step[0])

        @pl.when(sweep == 0)
        def _():
            gram_build[...] = build_gram_finish(gb0_recv, GB0)

        gram_hour = dot32(hour_cols[...], dot32(hour_rhs[:, 0:rank], inv_hour[...]))
        inverse = regularized_inverse(gram_build[...] * gram_hour)
        inv_sample[...] = inverse
        parts = jnp.concatenate(low16(*split(inverse)), axis=0)[:, :rank]
        gram_part = jnp.zeros((rank, rank), jnp.float32)

        for order, steps in enumerate(((0,), (1, 3), (2,))):
            chunks = [(y - dy + 4) % 4 for dy in steps]
            columns = []
            for dy, chunk in zip(steps, chunks):
                finish_exchange(AG1 + dy, ag1_recv.at[pl.ds(0, 3 if dy == 0 else 4)])
                for m in range(2):
                    even = ag1_recv[chunk * 4 + 2 * m].astype(jnp.float32)
                    odd = ag1_recv[chunk * 4 + 2 * m + 1].astype(jnp.float32)
                    moved = pltpu.roll(jnp.where(low_lane, odd, even), 64, 1)
                    top = jnp.where(low_lane, even, moved)
                    low = jnp.where(low_lane, moved, odd)
                    columns.append(jnp.concatenate([top, low], axis=0).astype(jnp.bfloat16))
            solved = solve_columns(parts, jnp.concatenate(columns, axis=1))
            rows = [pl.ds(pl.multiple_of(chunk * 256, 256), 256) for chunk in chunks]
            if order < 2:
                gram_part = gram_part + dot16(solved, solved, NT)
            for k in range(hours):
                for j in range(0, n_j, tile):
                    block = jnp.concatenate([slab[k, rows_of, j : j + tile] for rows_of in rows], axis=0)
                    block = dot16(solved, block)
                    if order == 0:
                        mixed[k, :, j : j + tile] = block
                    else:
                        mixed[k, :, j : j + tile] += block

        cols = [jnp.broadcast_to(hour_cols[:, k : k + 1], (rank, 128)) for k in range(hours)]
        for s in range(n_smp):
            at = place(s) * 128
            block = cols[0] * mixed[0, :, at : at + 128]
            for k in range(1, hours):
                block = block + cols[k] * mixed[k, :, at : at + 128]
            rs2_send[s] = block.astype(rs2_send.dtype)
        rs2_recv[smp] = rs2_send[smp]
        start_exchange("smp", lambda peer: rs2_send.at[peer], rs2_recv.at[smp], lambda step: RS2)

        message = pack(gram_part + dot16(solved, solved, NT))
        gs_send[...] = message
        gs_recv[smp] = message
        start_exchange("smp", lambda peer: gs_send, gs_recv.at[smp], lambda step: GS)

        finish_exchange(RS2, rs2_recv.at[pl.ds(0, n_smp - 1)])
        total = rs2_recv[0].astype(jnp.float32)
        for s in range(1, n_smp):
            total = total + rs2_recv[s].astype(jnp.float32)
        b_slice[...] = total
        message = total.astype(jnp.bfloat16)
        ag2_send[...] = message
        ag2_recv[smp] = message
        start_exchange("smp", lambda peer: ag2_send, ag2_recv.at[smp], lambda step: AG2 + step[1])

        finish_exchange(GS, gs_recv.at[pl.ds(0, n_smp - 1)])
        gram_raw = gs_recv[0]
        for s in range(1, n_smp):
            gram_raw = gram_raw + gs_recv[s]
        gram_raw = unpack_twice(gram_raw)
        inv_row, inv_col = scales_of(gram_raw, samples_total)
        inv_s_row[...] = jnp.broadcast_to(inv_row, inv_s_row.shape)
        inv_s_col[...] = jnp.broadcast_to(inv_col, inv_s_col.shape)
        gram_sample[...] = gram_raw * (inv_col * inv_row)
        inverse = regularized_inverse(gram_sample[...] * gram_hour) * inv_row
        inv_build[...] = inverse
        parts = jnp.concatenate(low16(*split(inverse)), axis=0)[:, :rank]

        sums = [jnp.zeros((rank, 128), jnp.float32) for _ in range(hours)]
        gram_part = jnp.zeros((rank, rank), jnp.float32)
        before_last = sweep < SWEEPS - 1
        groups = [(z - dz + 4) % 4 for dz in (0, 1, 3, 2)]
        early = {k: groups[:1] for k in range(hours)}
        for order, dz in enumerate((0, 1, 3, 2)):
            finish_exchange(AG2 + dz, ag2_recv.at[pl.ds(0, 1 if dz == 0 else 2)])
            group = groups[order]
            solved = solve_columns(parts, gathered(group))
            factor[:, pl.ds(pl.multiple_of(group * 256, 256), 256)] = solved
            gram_part = gram_part + dot16(solved, solved, NT)
            wide = solved.astype(jnp.float32)
            for k in range(hours):
                terms = slices(mixed, (k, slice(None)), [group]) * wide
                sums[k] = sums[k] + (terms[:, :128] + terms[:, 128:])
            if order < 2:

                @pl.when(before_last)
                def _():
                    for k in range(hours):
                        if order < len(early[k]):
                            for i in range(0, n_i, tile):
                                block = project(k, i, [group])
                                if order == 0:
                                    partial[k, :, i : i + tile] = block
                                else:
                                    partial[k, :, i : i + tile] += block

        message = lane_sums(sums)
        p1_send[...] = message
        p1_recv[bld] = message
        start_exchange("bld", lambda peer: p1_send, p1_recv.at[bld], lambda step: P1)
        message = pack(gram_part)
        gp_send[...] = message
        start_exchange("partner", lambda peer: gp_send, gp_recv, lambda step: GP)

        def finish_project(k):
            left = groups[len(early[k]) :]
            for i in range(0, n_i, tile):
                scatter(k, i, partial[k, :, i : i + tile] + project(k, i, left))
            pair_start(k)

        @pl.when(before_last)
        def _():
            finish_project(0)

        finish_exchange(GP, gp_recv)
        message = gp_send[...] + gp_recv[...]
        gb_send[...] = message
        gb_recv[chip] = message
        start_exchange("like", lambda peer: gb_send, gb_recv.at[chip], lambda step: GB)

        @pl.when(before_last)
        def _():
            for k in range(1, hours):
                finish_project(k)
                pair_finish(k - 1)
            pair_finish(hours - 1)

        rows = p1_recv.shape[0]
        finish_exchange(P1, p1_recv.at[pl.ds(0, rows - 1)])
        total = p1_recv[0]
        for n in range(1, rows):
            total = total + p1_recv[n]
        p2_send[...] = total
        p2_recv[smp] = total
        start_exchange("smp", lambda peer: p2_send, p2_recv.at[smp], lambda step: P2)

        gram_raw = build_gram_finish(gb_recv, GB)
        inv_row, inv_col = scales_of(gram_raw, buildings_total)
        inv_b_col[...] = jnp.broadcast_to(inv_col, inv_b_col.shape)
        gram_build[...] = gram_raw * (inv_col * inv_row)
        inverse = regularized_inverse(gram_sample[...] * gram_build[...])
        inv_hour[...] = inverse
        one, two = left_parts(inverse)
        scale_row = inv_row * inv_s_row[0:1, :]

        planes = p2_recv.shape[0]
        finish_exchange(P2, p2_recv.at[pl.ds(0, planes - 1)])
        total = p2_recv[0]
        for n in range(1, planes):
            total = total + p2_recv[n]
        right = total * scale_row
        hour_rhs[...] = right
        high, middle, rest = split(right)
        low = low_lanes(pad)
        both = jnp.where(low, high, middle).astype(jnp.bfloat16)
        far = jnp.where(low, high, rest).astype(jnp.bfloat16)
        hour_cols[...] = dot16(one, jnp.concatenate([both, far], axis=1), NT) + dot16(two, both, NT)

    sample_out[...] = product(inv_sample[...], unpack_twice(s_slice[...]))[:, :rank] * inv_s_col[:, 0:1]
    build_out[...] = product(inv_build[...], b_slice[...]) * inv_b_col[:, 0:1]
    hour_out[...] = dot32(hour_rhs[:, 0:rank], inv_hour[:, 0:rank])[0:hours] * scale_up


def put_out(a_ref, b_ref, c_ref, a_out, b_out, c_out, sems):
    pairs = ((a_ref, a_out), (b_ref, b_out), (c_ref, c_out))
    copies = [pltpu.make_async_copy(x, y, sems.at[n]) for n, (x, y) in enumerate(pairs)]
    for copy in copies:
        copy.start()
    for copy in copies:
        copy.wait()


def local(tensor, building_factor, hour_weights):
    n_smp = lax.axis_size("smp")
    n_bld = lax.axis_size("bld")
    hours, n_i, n_j = tensor.shape
    rank = building_factor.shape[0]
    assert (n_smp, n_bld, rank, hours) == (8, 16, 64, 4)
    i_share, j_share = n_i // n_bld, n_j // n_smp
    assert (i_share, j_share) == (64, 128)
    f32, bf16 = jnp.float32, jnp.bfloat16
    body = functools.partial(kernel, n_smp, n_bld, n_i * n_smp, n_j * n_bld)
    vmem = pl.BlockSpec(memory_space=pltpu.VMEM)
    pad = 8
    results = pl.pallas_call(
        body,
        out_shape=(
            jax.ShapeDtypeStruct((rank, i_share), f32),
            jax.ShapeDtypeStruct((rank, j_share), f32),
            jax.ShapeDtypeStruct((hours, rank), f32),
        ),
        in_specs=[pl.BlockSpec(memory_space=pl.ANY), vmem, vmem],
        out_specs=(vmem, vmem, vmem),
        scratch_shapes=[
            pltpu.VMEM((hours, n_i, n_j), bf16),
            pltpu.VMEM((hours, rank, n_j), f32),
            pltpu.VMEM((hours, rank, n_i), f32),
            pltpu.VMEM((rank, n_j), bf16),
            pltpu.VMEM((hours, n_bld // 2, rank // 2, 2 * i_share), f32),
            pltpu.VMEM((hours, n_bld // 2, rank // 2, 2 * i_share), bf16),
            pltpu.VMEM((hours, n_bld // 2, rank // 2, 2 * i_share), bf16),
            pltpu.VMEM((rank // 2, 2 * rank), f32),
            pltpu.VMEM((rank // 2, 2 * rank), f32),
            pltpu.VMEM((rank // 2, 2 * i_share), f32),
            pltpu.VMEM((rank, j_share), f32),
            pltpu.VMEM((rank, 2 * rank), f32),
            pltpu.VMEM((rank, 2 * rank), f32),
            pltpu.VMEM((rank, 2 * rank), f32),
            pltpu.VMEM((rank, 2 * rank), f32),
            pltpu.VMEM((rank, 2 * rank), f32),
            pltpu.VMEM((pad, 2 * rank), f32),
            pltpu.VMEM((rank, pad), f32),
            pltpu.VMEM((rank, pad), f32),
            pltpu.VMEM((pad, 2 * rank), f32),
            pltpu.VMEM((rank, pad), f32),
            pltpu.VMEM((hours, n_bld // 2, rank // 2, 2 * i_share), bf16),
            pltpu.VMEM((hours, n_bld // 2, rank // 2, 2 * i_share), bf16),
            pltpu.VMEM((rank // 2, 2 * i_share), bf16),
            pltpu.VMEM((n_bld, rank // 2, 2 * i_share), bf16),
            pltpu.VMEM((rank // 2, 2 * rank), f32),
            pltpu.VMEM((n_smp, rank // 2, 2 * rank), f32),
            pltpu.VMEM((n_smp, rank, j_share), bf16),
            pltpu.VMEM((n_smp, rank, j_share), bf16),
            pltpu.VMEM((rank, j_share), bf16),
            pltpu.VMEM((n_smp, rank, j_share), bf16),
            pltpu.VMEM((rank // 2, 2 * rank), f32),
            pltpu.VMEM((n_bld // 2, rank // 2, 2 * rank), f32),
            pltpu.VMEM((rank // 2, 2 * rank), f32),
            pltpu.VMEM((n_bld, rank // 2, 2 * rank), f32),
            pltpu.VMEM((pad, 2 * rank), f32),
            pltpu.VMEM((n_bld, pad, 2 * rank), f32),
            pltpu.VMEM((pad, 2 * rank), f32),
            pltpu.VMEM((n_smp, pad, 2 * rank), f32),
            pltpu.SemaphoreType.DMA((hours, n_smp)),
            pltpu.SemaphoreType.DMA((COUNT,)),
            pltpu.SemaphoreType.DMA((COUNT,)),
        ],
        compiler_params=pltpu.CompilerParams(
            collective_id=0, has_side_effects=True, vmem_limit_bytes=60 * 1024 * 1024
        ),
        name="als_sweeps",
    )(tensor, building_factor, hour_weights)
    return pl.pallas_call(
        put_out,
        out_shape=tuple(jax.ShapeDtypeStruct(x.shape, x.dtype) for x in results),
        in_specs=[vmem] * 3,
        out_specs=(pl.BlockSpec(memory_space=pl.ANY),) * 3,
        scratch_shapes=[pltpu.SemaphoreType.DMA((3,))],
        name="put_out",
    )(*results)


def solution(mesh):
    in_specs = (P(None, "smp", "bld"), P(None, "bld"), P())
    out_specs = (P(None, ("smp", "bld")), P(None, ("bld", "smp")), P())
    return jax.shard_map(local, mesh=mesh, in_specs=in_specs, out_specs=out_specs, check_vma=False)
```

```python
import functools
import math

import jax
import jax.numpy as jnp
from jax import lax
from jax.experimental import pallas as pl
from jax.experimental.pallas import tpu as pltpu
from jax.sharding import PartitionSpec as P

SWEEPS = 5
EPSILON = 1e-06
RIDGE_SHARE = 0.05
HIGHEST = lax.Precision.HIGHEST
MESH = pl.DeviceIdType.MESH
NT = (((1,), (1,)), ((), ()))
NN = (((1,), (0,)), ((), ()))

BLD_STEPS = [
    (dy, dx, dc) for dy in (2, 1, 3, 0) for dx in (1, 0) for dc in (1, 0) if (dy, dx, dc) != (0, 0, 0)
]
SMP_STEPS = [(dx, dz) for dz in (2, 1, 3, 0) for dx in (1, 0) if (dx, dz) != (0, 0)]


def dot32(a, b, dims=NN):
    return lax.dot_general(a, b, dims, precision=HIGHEST, preferred_element_type=jnp.float32)


def dot16(a, b, dims=NN):
    return lax.dot_general(a, b, dims, preferred_element_type=jnp.float32)


def identity(n):
    rows = lax.broadcasted_iota(jnp.int32, (n, n), 0)
    cols = lax.broadcasted_iota(jnp.int32, (n, n), 1)
    return (rows == cols).astype(jnp.float32)


def pack(square):
    half = square.shape[0] // 2
    return jnp.concatenate([square[:half], square[half:]], axis=1)


def low_lanes(rows):
    return lax.broadcasted_iota(jnp.int32, (rows, 128), 1) < 64


def unpack_twice(packed):
    turned = pltpu.roll(packed, 64, 1)
    low = low_lanes(packed.shape[0])
    return jnp.concatenate([jnp.where(low, packed, turned), jnp.where(low, turned, packed)], axis=0)


def identity_twice(n):
    rows = lax.broadcasted_iota(jnp.int32, (n, 2 * n), 0)
    cols = lax.broadcasted_iota(jnp.int32, (n, 2 * n), 1)
    return ((cols == rows) | (cols == rows + n)).astype(jnp.float32)


def split(x):
    high = x.astype(jnp.bfloat16).astype(jnp.float32)
    rest = x - high
    middle = rest.astype(jnp.bfloat16).astype(jnp.float32)
    return high, middle, rest - middle


def low16(*arrays):
    return [array.astype(jnp.bfloat16) for array in arrays]


def left_parts(a):
    high, middle, rest = split(a)
    low = low_lanes(a.shape[0])
    one = jnp.concatenate(low16(high, jnp.where(low, middle, high)), axis=1)
    two = jnp.where(low, rest, middle).astype(jnp.bfloat16)
    return one, two


def product(a, b):
    one, two = left_parts(a)
    high, middle, rest = low16(*split(b))
    return dot16(one, jnp.concatenate([high, middle, high, rest], axis=0)) + dot16(
        two, jnp.concatenate([high, middle], axis=0)
    )


def regularized_inverse(gram):
    n = gram.shape[0]
    eye = identity_twice(n)
    mean = jnp.sum(jnp.sum(gram * eye, axis=0, keepdims=True), axis=1, keepdims=True) / (2 * n)
    scale = 2.0 / ((n + 2 * RIDGE_SHARE) * mean)
    t = scale * (gram + RIDGE_SHARE * mean * eye)
    y = None
    spread = n / (n + 2 * RIDGE_SHARE)
    steps = 8
    for step in range(steps):
        spread = spread * spread / (2.0 - spread * spread)
        gain = 1.0 + spread
        factor = gain * (2.0 * eye - t)
        if step == 0:
            y = factor
            t = product(t, factor)
        elif step < steps - 1:
            both = product(jnp.concatenate([y, t], axis=0), factor)
            y, t = both[:n], both[n:]
        else:
            y = product(y, factor)
    return scale * y


def scales_of(gram_raw, count):
    n = gram_raw.shape[0]
    diagonal = gram_raw * identity_twice(n)
    inv_row = 1.0 / jnp.sqrt(jnp.sum(diagonal, axis=0, keepdims=True) / count + EPSILON)
    inv_col = 1.0 / jnp.sqrt(jnp.sum(diagonal, axis=1, keepdims=True) / (2 * count) + EPSILON)
    return inv_row, inv_col


RS1, AG1, AG2, PAIR, GS, RS2, GB, P1, P2, GB0, GP, COUNT = 0, 4, 8, 12, 16, 17, 18, 19, 20, 21, 22, 23


def kernel(
    n_smp, n_bld, samples_total, buildings_total,
    tensor_ref, build_ref, hour_ref,
    sample_out, build_out, hour_out,
    slab, mixed, partial, factor, own, pair_send, pair_recv, gp_send, gp_recv, s_slice, b_slice,
    gram_build, gram_sample, inv_sample, inv_build, inv_hour, hour_rhs, hour_cols, inv_b_col, inv_s_row, inv_s_col,
    rs1_send, rs1_recv, ag1_send, ag1_recv, gs_send, gs_recv,
    rs2_send, rs2_recv, ag2_send, ag2_recv, gb_send, gb_recv, gb0_send, gb0_recv, p1_send, p1_recv, p2_send, p2_recv,
    load_sem, send_sems, recv_sems,
):
    hours, n_i, n_j = slab.shape
    rank = build_ref.shape[0]
    half = rank // 2
    scale_up = math.sqrt(samples_total * buildings_total)
    smp = lax.axis_index("smp")
    bld = lax.axis_index("bld")
    core = bld % 2
    x_hi = (bld // 2) % 2
    y = bld // 4
    z = smp % 4
    x_lo = smp // 4

    def bld_peer(step):
        dy, dx, dc = step
        return ((y + dy) % 4) * 4 + ((x_hi + dx) % 2) * 2 + (core + dc) % 2

    def smp_peer(step):
        dx, dz = step
        return ((x_lo + dx) % 2) * 4 + (z + dz) % 4

    bld_peers = [bld_peer(step) for step in BLD_STEPS]
    like_steps = [step for step in BLD_STEPS if step[2] == 0]
    like_peers = [bld_peer(step) for step in like_steps]
    partner = bld_peer((0, 0, 1))
    chip = bld // 2
    n_chip = n_bld // 2
    smp_peers = [smp_peer(step) for step in SMP_STEPS]

    def start_exchange(axis, piece_of, place, sem_of):
        if axis == "like":
            peers, steps, axis = like_peers, like_steps, "bld"
        elif axis == "partner":
            peers, steps, axis = [partner], [(0, 0, 1)], "bld"
        elif axis == "bld":
            peers, steps = bld_peers, BLD_STEPS
        else:
            peers, steps = smp_peers, SMP_STEPS
        for peer, step in zip(peers, steps):
            pltpu.make_async_remote_copy(
                src_ref=piece_of(peer),
                dst_ref=place,
                send_sem=send_sems.at[sem_of(step)],
                recv_sem=recv_sems.at[sem_of(step)],
                device_id={axis: peer},
                device_id_type=MESH,
            ).start()

    def finish_exchange(sem, pieces):
        done = pltpu.make_async_remote_copy(
            src_ref=pieces,
            dst_ref=pieces,
            send_sem=send_sems.at[sem],
            recv_sem=recv_sems.at[sem],
            device_id={"bld": bld_peers[0]},
            device_id_type=MESH,
        )
        done.wait_recv()
        done.wait_send()

    barrier = pltpu.get_barrier_semaphore()
    for peer in bld_peers:
        pl.semaphore_signal(barrier, inc=1, device_id={"bld": peer}, device_id_type=MESH)
    for peer in smp_peers:
        pl.semaphore_signal(barrier, inc=1, device_id={"smp": peer}, device_id_type=MESH)

    def place(s):
        return (s % 4) * 2 + s // 4

    def load(k, s):
        from_ref = tensor_ref.at[k, :, s * 128 : (s + 1) * 128]
        to_ref = slab.at[k, :, place(s) * 128 : (place(s) + 1) * 128]
        return pltpu.make_async_copy(from_ref, to_ref, load_sem.at[k, s])

    for k in range(hours):
        for s in range(n_smp):
            load(k, s).start()

    low_lane = low_lanes(half)
    tile = 512

    def scatter(k, i, block):
        for m in range(tile // 128):
            top, low = block[:half, m * 128 : (m + 1) * 128], block[half:, m * 128 : (m + 1) * 128]
            moved = pltpu.roll(jnp.where(low_lane, low, top), 64, 1)
            even = jnp.where(low_lane, top, moved)
            odd = jnp.where(low_lane, moved, low)
            own[k, i // 128 + m] = jnp.where(core == 0, even, odd)
            pair_send[k, i // 128 + m] = jnp.where(core == 0, odd, even).astype(pair_send.dtype)

    def pair_start(k):
        start_exchange("partner", lambda peer: pair_send.at[k], pair_recv.at[k], lambda step: PAIR + k)

    def pair_finish(k):
        finish_exchange(PAIR + k, pair_recv.at[k])
        for c in range(n_chip):
            rs1_send[k, c] = (own[k, c] + pair_recv[k, c].astype(jnp.float32)).astype(rs1_send.dtype)
        rs1_recv[k, chip] = rs1_send[k, chip]
        start_exchange("like", lambda peer: rs1_send.at[k, peer // 2], rs1_recv.at[k, chip], lambda step: RS1 + k)

    def slices(ref, index, groups):
        parts = [ref[index + (pl.ds(pl.multiple_of(group * 256, 256), 256),)] for group in groups]
        return parts[0] if len(parts) == 1 else jnp.concatenate(parts, axis=-1)

    def gathered(group):
        return jnp.concatenate([ag2_recv[group], ag2_recv[4 + group]], axis=1)

    def solve_columns(parts, columns):
        solved = dot16(parts, columns)
        solved = solved[:rank] + (solved[rank : 2 * rank] + solved[2 * rank :])
        return solved.astype(jnp.bfloat16)

    def project(k, i, groups):
        return dot16(slices(factor, (slice(None),), groups), slices(slab, (k, slice(i, i + tile)), groups), NT)

    def build_gram_start(gram, send, recv, sem):
        message = pack(gram)
        send[...] = message
        recv[bld] = message
        start_exchange("bld", lambda peer: send, recv.at[bld], lambda step: sem)

    def build_gram_finish(recv, sem):
        others = recv.shape[0] - 1
        finish_exchange(sem, recv.at[pl.ds(0, others)])
        total = recv[0]
        for b in range(1, others + 1):
            total = total + recv[b]
        return unpack_twice(total)

    pad = hour_rhs.shape[0]
    pick_rows = lax.broadcasted_iota(jnp.int32, (pad, 128), 0)
    quarter = lax.broadcasted_iota(jnp.int32, (pad, 128), 1) // 32
    held = jnp.where(quarter == 0, 2, jnp.where(quarter == 1, 0, jnp.where(quarter == 2, 3, 1)))
    pick = (pick_rows == held).astype(jnp.bfloat16)

    def lane_sums(sums):
        low = low_lanes(rank)
        folded = [x + pltpu.roll(x, 64, 1) for x in sums]
        first = jnp.where(low, folded[0], folded[1])
        second = jnp.where(low, folded[2], folded[3])
        first = first + pltpu.roll(first, 32, 1)
        second = second + pltpu.roll(second, 96, 1)
        upper = (lax.broadcasted_iota(jnp.int32, (rank, 128), 1) // 32) % 2 == 1
        parts = low16(*split(jnp.where(upper, first, second)))
        rows = dot16(jnp.concatenate([pick] * 3, axis=1), jnp.concatenate(parts, axis=1), NT)
        return jnp.concatenate([rows, rows], axis=1)

    hour_rhs[...] = jnp.zeros_like(hour_rhs)
    hour_rhs[0:hours, 0:rank] = hour_ref[...] / scale_up
    inv_hour[...] = identity_twice(rank)
    hour_cols[...] = dot32(identity(rank), hour_rhs[:, 0:rank], NT)
    inv_b_col[...] = jnp.ones_like(inv_b_col)
    order_of = sorted(range(n_smp), key=place)
    start_factor = jnp.concatenate(
        [build_ref[:, s * 128 : (s + 1) * 128] for s in order_of], axis=1
    ).astype(jnp.bfloat16)
    for k in range(hours):
        for s in range(n_smp):
            load(k, s).wait()
        for i in range(0, n_i, tile):
            scatter(k, i, dot16(start_factor, slab[k, i : i + tile, :], NT))
        if k == 1:
            pl.semaphore_wait(barrier, n_bld + n_smp - 2)
            pair_start(0)
        if k >= 1:
            pair_start(k)
            pair_finish(k - 1)
    pair_finish(hours - 1)
    build_gram_start(dot32(build_ref[...], build_ref[...], NT), gb0_send, gb0_recv, GB0)

    @pl.loop(0, SWEEPS)
    def _(sweep):
        for k in range(hours):
            finish_exchange(RS1 + k, rs1_recv.at[k, pl.ds(0, n_chip - 1)])
        right = None
        for k in range(hours):
            col = hour_cols[:, k : k + 1] * inv_b_col[:, 0:1]
            both = jnp.where(
                low_lane,
                jnp.broadcast_to(col[:half], (half, 128)),
                jnp.broadcast_to(col[half:], (half, 128)),
            )
            total = rs1_recv[k, 0].astype(jnp.float32)
            for c in range(1, n_chip):
                total = total + rs1_recv[k, c].astype(jnp.float32)
            right = both * total if right is None else right + both * total
        s_slice[...] = right
        message = right.astype(jnp.bfloat16)
        ag1_send[...] = message
        ag1_recv[bld] = message
        start_exchange("bld", lambda peer: ag1_send, ag1_recv.at[bld], lambda step: AG1 + step[0])

        @pl.when(sweep == 0)
        def _():
            gram_build[...] = build_gram_finish(gb0_recv, GB0)

        gram_hour = dot32(hour_cols[...], dot32(hour_rhs[:, 0:rank], inv_hour[...]))
        inverse = regularized_inverse(gram_build[...] * gram_hour)
        inv_sample[...] = inverse
        parts = jnp.concatenate(low16(*split(inverse)), axis=0)[:, :rank]
        gram_part = jnp.zeros((rank, rank), jnp.float32)

        for order, steps in enumerate(((0,), (1, 3), (2,))):
            chunks = [(y - dy + 4) % 4 for dy in steps]
            columns = []
            for dy, chunk in zip(steps, chunks):
                finish_exchange(AG1 + dy, ag1_recv.at[pl.ds(0, 3 if dy == 0 else 4)])
                for m in range(2):
                    even = ag1_recv[chunk * 4 + 2 * m].astype(jnp.float32)
                    odd = ag1_recv[chunk * 4 + 2 * m + 1].astype(jnp.float32)
                    moved = pltpu.roll(jnp.where(low_lane, odd, even), 64, 1)
                    top = jnp.where(low_lane, even, moved)
                    low = jnp.where(low_lane, moved, odd)
                    columns.append(jnp.concatenate([top, low], axis=0).astype(jnp.bfloat16))
            solved = solve_columns(parts, jnp.concatenate(columns, axis=1))
            rows = [pl.ds(pl.multiple_of(chunk * 256, 256), 256) for chunk in chunks]
            if order < 2:
                gram_part = gram_part + dot16(solved, solved, NT)
            for k in range(hours):
                for j in range(0, n_j, tile):
                    block = jnp.concatenate([slab[k, rows_of, j : j + tile] for rows_of in rows], axis=0)
                    block = dot16(solved, block)
                    if order == 0:
                        mixed[k, :, j : j + tile] = block
                    else:
                        mixed[k, :, j : j + tile] += block

        cols = [jnp.broadcast_to(hour_cols[:, k : k + 1], (rank, 128)) for k in range(hours)]
        for s in range(n_smp):
            at = place(s) * 128
            block = cols[0] * mixed[0, :, at : at + 128]
            for k in range(1, hours):
                block = block + cols[k] * mixed[k, :, at : at + 128]
            rs2_send[s] = block.astype(rs2_send.dtype)
        rs2_recv[smp] = rs2_send[smp]
        start_exchange("smp", lambda peer: rs2_send.at[peer], rs2_recv.at[smp], lambda step: RS2)

        message = pack(gram_part + dot16(solved, solved, NT))
        gs_send[...] = message
        gs_recv[smp] = message
        start_exchange("smp", lambda peer: gs_send, gs_recv.at[smp], lambda step: GS)

        finish_exchange(RS2, rs2_recv.at[pl.ds(0, n_smp - 1)])
        total = rs2_recv[0].astype(jnp.float32)
        for s in range(1, n_smp):
            total = total + rs2_recv[s].astype(jnp.float32)
        b_slice[...] = total
        message = total.astype(jnp.bfloat16)
        ag2_send[...] = message
        ag2_recv[smp] = message
        start_exchange("smp", lambda peer: ag2_send, ag2_recv.at[smp], lambda step: AG2 + step[1])

        finish_exchange(GS, gs_recv.at[pl.ds(0, n_smp - 1)])
        gram_raw = gs_recv[0]
        for s in range(1, n_smp):
            gram_raw = gram_raw + gs_recv[s]
        gram_raw = unpack_twice(gram_raw)
        inv_row, inv_col = scales_of(gram_raw, samples_total)
        inv_s_row[...] = jnp.broadcast_to(inv_row, inv_s_row.shape)
        inv_s_col[...] = jnp.broadcast_to(inv_col, inv_s_col.shape)
        gram_sample[...] = gram_raw * (inv_col * inv_row)
        inverse = regularized_inverse(gram_sample[...] * gram_hour) * inv_row
        inv_build[...] = inverse
        parts = jnp.concatenate(low16(*split(inverse)), axis=0)[:, :rank]

        sums = [jnp.zeros((rank, 128), jnp.float32) for _ in range(hours)]
        gram_part = jnp.zeros((rank, rank), jnp.float32)
        before_last = sweep < SWEEPS - 1
        groups = [(z - dz + 4) % 4 for dz in (0, 1, 3, 2)]
        early = {k: groups[:1] if k < 2 else [] for k in range(hours)}
        for order, dz in enumerate((0, 1, 3, 2)):
            finish_exchange(AG2 + dz, ag2_recv.at[pl.ds(0, 1 if dz == 0 else 2)])
            group = groups[order]
            solved = solve_columns(parts, gathered(group))
            factor[:, pl.ds(pl.multiple_of(group * 256, 256), 256)] = solved
            gram_part = gram_part + dot16(solved, solved, NT)
            wide = solved.astype(jnp.float32)
            for k in range(hours):
                terms = slices(mixed, (k, slice(None)), [group]) * wide
                sums[k] = sums[k] + (terms[:, :128] + terms[:, 128:])
            if order < 1:

                @pl.when(before_last)
                def _():
                    for k in range(hours):
                        if order < len(early[k]):
                            for i in range(0, n_i, tile):
                                block = project(k, i, [group])
                                if order == 0:
                                    partial[k, :, i : i + tile] = block
                                else:
                                    partial[k, :, i : i + tile] += block

        message = lane_sums(sums)
        p1_send[...] = message
        p1_recv[bld] = message
        start_exchange("bld", lambda peer: p1_send, p1_recv.at[bld], lambda step: P1)
        message = pack(gram_part)
        gp_send[...] = message
        start_exchange("partner", lambda peer: gp_send, gp_recv, lambda step: GP)

        def finish_project(k):
            left = groups[len(early[k]) :]
            for i in range(0, n_i, tile):
                block = project(k, i, left)
                scatter(k, i, partial[k, :, i : i + tile] + block if early[k] else block)
            pair_start(k)

        @pl.when(before_last)
        def _():
            finish_project(0)

        finish_exchange(GP, gp_recv)
        message = gp_send[...] + gp_recv[...]
        gb_send[...] = message
        gb_recv[chip] = message
        start_exchange("like", lambda peer: gb_send, gb_recv.at[chip], lambda step: GB)

        @pl.when(before_last)
        def _():
            for k in range(1, hours):
                finish_project(k)
                pair_finish(k - 1)
            pair_finish(hours - 1)

        rows = p1_recv.shape[0]
        finish_exchange(P1, p1_recv.at[pl.ds(0, rows - 1)])
        total = p1_recv[0]
        for n in range(1, rows):
            total = total + p1_recv[n]
        p2_send[...] = total
        p2_recv[smp] = total
        start_exchange("smp", lambda peer: p2_send, p2_recv.at[smp], lambda step: P2)

        gram_raw = build_gram_finish(gb_recv, GB)
        inv_row, inv_col = scales_of(gram_raw, buildings_total)
        inv_b_col[...] = jnp.broadcast_to(inv_col, inv_b_col.shape)
        gram_build[...] = gram_raw * (inv_col * inv_row)
        inverse = regularized_inverse(gram_sample[...] * gram_build[...])
        inv_hour[...] = inverse
        one, two = left_parts(inverse)
        scale_row = inv_row * inv_s_row[0:1, :]

        planes = p2_recv.shape[0]
        finish_exchange(P2, p2_recv.at[pl.ds(0, planes - 1)])
        total = p2_recv[0]
        for n in range(1, planes):
            total = total + p2_recv[n]
        right = total * scale_row
        hour_rhs[...] = right
        high, middle, rest = split(right)
        low = low_lanes(pad)
        both = jnp.where(low, high, middle).astype(jnp.bfloat16)
        far = jnp.where(low, high, rest).astype(jnp.bfloat16)
        hour_cols[...] = dot16(one, jnp.concatenate([both, far], axis=1), NT) + dot16(two, both, NT)

    sample_out[...] = product(inv_sample[...], unpack_twice(s_slice[...]))[:, :rank] * inv_s_col[:, 0:1]
    build_out[...] = product(inv_build[...], b_slice[...]) * inv_b_col[:, 0:1]
    hour_out[...] = dot32(hour_rhs[:, 0:rank], inv_hour[:, 0:rank])[0:hours] * scale_up


def put_out(a_ref, b_ref, c_ref, a_out, b_out, c_out, sems):
    pairs = ((a_ref, a_out), (b_ref, b_out), (c_ref, c_out))
    copies = [pltpu.make_async_copy(x, y, sems.at[n]) for n, (x, y) in enumerate(pairs)]
    for copy in copies:
        copy.start()
    for copy in copies:
        copy.wait()


def local(tensor, building_factor, hour_weights):
    n_smp = lax.axis_size("smp")
    n_bld = lax.axis_size("bld")
    hours, n_i, n_j = tensor.shape
    rank = building_factor.shape[0]
    assert (n_smp, n_bld, rank, hours) == (8, 16, 64, 4)
    i_share, j_share = n_i // n_bld, n_j // n_smp
    assert (i_share, j_share) == (64, 128)
    f32, bf16 = jnp.float32, jnp.bfloat16
    body = functools.partial(kernel, n_smp, n_bld, n_i * n_smp, n_j * n_bld)
    vmem = pl.BlockSpec(memory_space=pltpu.VMEM)
    pad = 8
    results = pl.pallas_call(
        body,
        out_shape=(
            jax.ShapeDtypeStruct((rank, i_share), f32),
            jax.ShapeDtypeStruct((rank, j_share), f32),
            jax.ShapeDtypeStruct((hours, rank), f32),
        ),
        in_specs=[pl.BlockSpec(memory_space=pl.ANY), vmem, vmem],
        out_specs=(vmem, vmem, vmem),
        scratch_shapes=[
            pltpu.VMEM((hours, n_i, n_j), bf16),
            pltpu.VMEM((hours, rank, n_j), f32),
            pltpu.VMEM((hours, rank, n_i), f32),
            pltpu.VMEM((rank, n_j), bf16),
            pltpu.VMEM((hours, n_bld // 2, rank // 2, 2 * i_share), f32),
            pltpu.VMEM((hours, n_bld // 2, rank // 2, 2 * i_share), bf16),
            pltpu.VMEM((hours, n_bld // 2, rank // 2, 2 * i_share), bf16),
            pltpu.VMEM((rank // 2, 2 * rank), f32),
            pltpu.VMEM((rank // 2, 2 * rank), f32),
            pltpu.VMEM((rank // 2, 2 * i_share), f32),
            pltpu.VMEM((rank, j_share), f32),
            pltpu.VMEM((rank, 2 * rank), f32),
            pltpu.VMEM((rank, 2 * rank), f32),
            pltpu.VMEM((rank, 2 * rank), f32),
            pltpu.VMEM((rank, 2 * rank), f32),
            pltpu.VMEM((rank, 2 * rank), f32),
            pltpu.VMEM((pad, 2 * rank), f32),
            pltpu.VMEM((rank, pad), f32),
            pltpu.VMEM((rank, pad), f32),
            pltpu.VMEM((pad, 2 * rank), f32),
            pltpu.VMEM((rank, pad), f32),
            pltpu.VMEM((hours, n_bld // 2, rank // 2, 2 * i_share), bf16),
            pltpu.VMEM((hours, n_bld // 2, rank // 2, 2 * i_share), bf16),
            pltpu.VMEM((rank // 2, 2 * i_share), bf16),
            pltpu.VMEM((n_bld, rank // 2, 2 * i_share), bf16),
            pltpu.VMEM((rank // 2, 2 * rank), f32),
            pltpu.VMEM((n_smp, rank // 2, 2 * rank), f32),
            pltpu.VMEM((n_smp, rank, j_share), bf16),
            pltpu.VMEM((n_smp, rank, j_share), bf16),
            pltpu.VMEM((rank, j_share), bf16),
            pltpu.VMEM((n_smp, rank, j_share), bf16),
            pltpu.VMEM((rank // 2, 2 * rank), f32),
            pltpu.VMEM((n_bld // 2, rank // 2, 2 * rank), f32),
            pltpu.VMEM((rank // 2, 2 * rank), f32),
            pltpu.VMEM((n_bld, rank // 2, 2 * rank), f32),
            pltpu.VMEM((pad, 2 * rank), f32),
            pltpu.VMEM((n_bld, pad, 2 * rank), f32),
            pltpu.VMEM((pad, 2 * rank), f32),
            pltpu.VMEM((n_smp, pad, 2 * rank), f32),
            pltpu.SemaphoreType.DMA((hours, n_smp)),
            pltpu.SemaphoreType.DMA((COUNT,)),
            pltpu.SemaphoreType.DMA((COUNT,)),
        ],
        compiler_params=pltpu.CompilerParams(
            collective_id=0, has_side_effects=True, vmem_limit_bytes=60 * 1024 * 1024
        ),
        name="als_sweeps",
    )(tensor, building_factor, hour_weights)
    return pl.pallas_call(
        put_out,
        out_shape=tuple(jax.ShapeDtypeStruct(x.shape, x.dtype) for x in results),
        in_specs=[vmem] * 3,
        out_specs=(pl.BlockSpec(memory_space=pl.ANY),) * 3,
        scratch_shapes=[pltpu.SemaphoreType.DMA((3,))],
        name="put_out",
    )(*results)


def solution(mesh):
    in_specs = (P(None, "smp", "bld"), P(None, "bld"), P())
    out_specs = (P(None, ("smp", "bld")), P(None, ("bld", "smp")), P())
    return jax.shard_map(local, mesh=mesh, in_specs=in_specs, out_specs=out_specs, check_vma=False)
```
